32 devices in a mesh: dp: 8 (over y, x, core), tensor: 4 (over z).
Axes of the slice: x: 2, y: 2, z: 4, core: 2. Of those that a mesh axis runs over, the one named last changes fastest.
Arguments:
- tokens: bfloat16 [2, 8192, 768], P(None, ('dp', 'tensor')), may hold values from -6 to 6
- lengths: int32 [2, 8, 3], P(None, 'dp'), may hold values from 1 to 768, 1024 in all within a row
- dealing: int32 [2, 8, 8], P(None, 'dp'), may hold values from 0 to 7, each once within a row
- cotangent: bfloat16 [2, 8192, 768], P(None, ('dp', 'tensor')), may hold values from -6 to 6
- pre_gain: bfloat16 [768], P(('dp', 'tensor')), may hold values from 0.5 to 1.5
- w_z: bfloat16 [768, 1536], P('dp', 'tensor'), may hold values from -0.21875 to 0.21875
- w_x: bfloat16 [768, 1536], P('dp', 'tensor'), may hold values from -0.21875 to 0.21875
- w_bc: bfloat16 [768, 256], P(('dp', 'tensor')), may hold values from -0.21875 to 0.21875
- w_dt: bfloat16 [768, 24], P('dp', 'tensor'), may hold values from -0.21875 to 0.21875
- conv_x: bfloat16 [4, 24, 64], P(None, 'tensor', 'dp'), may hold values from -3 to 3
- conv_bx: bfloat16 [24, 64], P('tensor', 'dp'), may hold values from -3 to 3
- conv_bc: bfloat16 [4, 256], P(None, ('dp', 'tensor')), may hold values from -3 to 3
- conv_bbc: bfloat16 [256], P(('dp', 'tensor')), may hold values from -3 to 3
- dt_bias: float32 [24], P('tensor'), may hold values from -6 to -2.5
- a_log: float32 [24], P('tensor'), may hold values from 0 to 2.77
- d_skip: float32 [24], P('tensor'), may hold values from 0.5 to 2
- norm_gain: bfloat16 [24, 64], P('tensor', 'dp'), may hold values from 0.5 to 1.5
- w_out: bfloat16 [1536, 768], P('tensor', 'dp'), may hold values from -0.15625 to 0.15625
Outputs:
- output: bfloat16 [2, 8192, 768], P(None, ('dp', 'tensor'))
- d_tokens: bfloat16 [2, 8192, 768], P(None, ('dp', 'tensor'))
- d_pre_gain: float32 [768], P(('dp', 'tensor'))
- d_w_z: float32 [768, 1536], P('dp', 'tensor')
- d_w_x: float32 [768, 1536], P('dp', 'tensor')
- d_w_bc: float32 [768, 256], P(('dp', 'tensor'))
- d_w_dt: float32 [768, 24], P('dp', 'tensor')
- d_conv_x: float32 [4, 24, 64], P(None, 'tensor', 'dp')
- d_conv_bx: float32 [24, 64], P('tensor', 'dp')
- d_conv_bc: float32 [4, 256], P(None, ('dp', 'tensor'))
- d_conv_bbc: float32 [256], P(('dp', 'tensor'))
- d_dt_bias: float32 [24], P('tensor')
- d_a_log: float32 [24], P('tensor')
- d_d_skip: float32 [24], P('tensor')
- d_norm_gain: float32 [24, 64], P('tensor', 'dp')
- d_w_out: float32 [1536, 768], P('tensor', 'dp')
The draws below stay inside these ranges and needn't reach their ends.
Inputs may be any that keep to these rules, and one draw needn't show every extreme that they name: Each bin's lengths sum to 1024; in each bin the largest is exactly 768.
All inputs are finite; a program needn't handle non-finite values.
Results may differ from the reference program's by a relative error of at most 0.013.
Values may be sent and summed in bfloat16 or wider, within the bound.
A program may use at most 128 MiB of HBM per device.

```python
import math
import jax
import jax.numpy as jnp
import numpy as np
from jax import lax

D = 768
HEADS = 24
HEAD_DIM = 64
STATE = 128
CONV = 4
BLOCK = 256
MICRO = 2
SEQS_BIN = 3
INNER = 1536
BIN = 1024
LONGEST = 768
BINS = 8
ROWS = 8192
PIECE = 32
N_DP = 8
N_TENSOR = 4


def levels(stream_key, dims, cuts, least, top_value):
    level = 1.0
    for axis_at, shards_of in cuts:
        draws = jax.random.uniform(jax.random.fold_in(jax.random.fold_in(stream_key, 6), axis_at), (shards_of,), jnp.float32, least / len(cuts), top_value / len(cuts))
        level = level * jnp.repeat(jnp.exp(draws), dims[axis_at] // shards_of).reshape((-1,) + (1,) * (len(dims) - 1 - axis_at))
    return level


def length_profile(count, total, most, slope):
    portions = [(1 << 20) // math.isqrt(grade ** slope) + 1 for grade in range(2, count + 1)]
    rest, given = total - most - (count - 1), [1] * (count - 1)
    while rest > 0:
        candidates = [i for i in range(count - 1) if given[i] < most]
        mass, remaining = sum([portions[i] for i in candidates]), rest
        for i in candidates:
            addition = min(most - given[i], max(1, remaining * portions[i] // mass), rest)
            given[i] = given[i] + addition
            rest = rest - addition
    return np.array([most] + given)


def uneven_parts(own_key, amount, total, reach, slope):
    if amount == 2:
        one = jax.random.randint(own_key, (), max(1, total - reach), min(reach, total - 1) + 1)
        return jnp.stack([one, total - one])
    tallies = jnp.asarray(length_profile(amount, total, reach, slope), jnp.int32)
    twos = (amount - 1) // 2
    giver, sink = tallies[1:1 + 2 * twos:2], tallies[2:2 + 2 * twos:2]
    room = jnp.minimum(giver - 1, reach - sink)
    moved = jax.random.randint(jax.random.fold_in(own_key, 1), (twos,), 0, 1 << 20) % (room + 1)
    tallies = tallies.at[1:1 + 2 * twos:2].set(giver - moved).at[2:2 + 2 * twos:2].set(sink + moved)
    return tallies[jax.random.permutation(jax.random.fold_in(own_key, 2), amount)]


def noise(rng, shape, scale, most, cuts=(), held_as=jnp.bfloat16):
    values = scale * jax.random.normal(rng, shape, jnp.float32)
    if cuts:
        values = values * levels(rng, shape, cuts, -0.22, 0.18)
    return jnp.clip(values, -most, most).astype(held_as)


def setup_inputs(seed: int = 0) -> dict:
    streams_of = jax.random.split(jax.random.key(seed), 19)
    return {
        "tokens": noise(streams_of[0], (MICRO, ROWS, D), 1.0, 6.0, ((1, 32),)),
        "lengths": jax.vmap(lambda own: uneven_parts(own, SEQS_BIN, BIN, LONGEST, 2))(jax.random.split(streams_of[1], MICRO * BINS)).reshape((MICRO, BINS, SEQS_BIN)).astype(jnp.int32),
        "dealing": jax.vmap(lambda own: jax.random.permutation(own, BINS))(jax.random.split(streams_of[2], MICRO * BINS)).reshape((MICRO, BINS, BINS)).astype(jnp.int32),
        "cotangent": noise(streams_of[3], (MICRO, ROWS, D), 1.0, 6.0, ((1, 32),)),
        "pre_gain": jnp.clip(1.0 + 0.1 * jax.random.normal(streams_of[4], (D,), jnp.float32), 0.5, 1.5).astype(jnp.bfloat16),
        "w_z": noise(streams_of[5], (D, INNER), D ** -0.5, 0.21875, ((0, 8), (1, 4))),
        "w_x": noise(streams_of[6], (D, INNER), D ** -0.5, 0.21875, ((0, 8), (1, 4))),
        "w_bc": noise(streams_of[7], (D, 2 * STATE), D ** -0.5, 0.21875, ((0, 32),)),
        "w_dt": noise(streams_of[8], (D, HEADS), D ** -0.5, 0.21875, ((0, 8), (1, 4))),
        "conv_x": noise(streams_of[9], (CONV, HEADS, HEAD_DIM), CONV ** -0.5, 3.0, ((1, 4), (2, 8))),
        "conv_bx": noise(streams_of[10], (HEADS, HEAD_DIM), 0.5, 3.0, ((0, 4), (1, 8))),
        "conv_bc": noise(streams_of[11], (CONV, 2 * STATE), CONV ** -0.5, 3.0, ((1, 32),)),
        "conv_bbc": noise(streams_of[12], (2 * STATE,), 0.5, 3.0, ((0, 32),)),
        "dt_bias": jnp.clip(-6.0 + 3.5 * jax.random.uniform(streams_of[13], (HEADS,), jnp.float32) ** levels(streams_of[13], (HEADS,), ((0, 4),), -0.2, 0.2), -6.0, -2.5),
        "a_log": jnp.clip(2.77 * jax.random.uniform(streams_of[14], (HEADS,), jnp.float32) ** levels(streams_of[14], (HEADS,), ((0, 4),), -0.2, 0.2), 0.0, 2.77),
        "d_skip": jnp.clip(0.5 + 1.5 * jax.random.uniform(streams_of[15], (HEADS,), jnp.float32) ** levels(streams_of[15], (HEADS,), ((0, 4),), -0.2, 0.2), 0.5, 2.0),
        "norm_gain": jnp.clip(1.0 + 0.1 * jax.random.normal(streams_of[16], (HEADS, HEAD_DIM), jnp.float32), 0.5, 1.5).astype(jnp.bfloat16),
        "w_out": noise(streams_of[17], (INNER, D), INNER ** -0.5, 0.15625, ((0, 4), (1, 8))),
    }


epsilon = 1e-05
highest = lax.Precision.HIGHEST

@jax.custom_vjp
def low(v):
    return lax.optimization_barrier(v.astype(jnp.bfloat16)).astype(jnp.float32)

@jax.custom_vjp
def low_back(v):
    return v

def low_keep(v):
    return (low(v), None)

def low_pass(kept, grad):
    return (grad,)

def back_keep(v):
    return (v, None)

def back_low(kept, grad):
    return (low(grad),)
low.defvjp(low_keep, low_pass)
low_back.defvjp(back_keep, back_low)

def product(left, right):
    return jnp.dot(left, right, precision=highest, preferred_element_type=jnp.float32)

def segment_ids(lengths, length):
    bounds = jnp.cumsum(lengths).astype(jnp.int32)
    places = jnp.arange(length, dtype=jnp.int32)
    return lax.optimization_barrier(jnp.sum((places[:, None] >= bounds[None, :]).astype(jnp.int32), axis=1)).astype(jnp.int32)

def causal_conv(values, kernel, bias, segments):
    taps_count = kernel.shape[0]
    length = values.shape[0]
    padded = jnp.concatenate([jnp.zeros((taps_count - 1, values.shape[1]), values.dtype), values], axis=0)
    padded_seg = jnp.concatenate([jnp.full((taps_count - 1,), -1, dtype=jnp.int32), segments], axis=0)
    result = jnp.zeros_like(values) + bias[None, :]
    for offset in range(taps_count):
        shifted = lax.slice_in_dim(padded, offset, offset + length, axis=0)
        matched = (lax.slice_in_dim(padded_seg, offset, offset + length, axis=0) == segments).astype(values.dtype)
        result = result + kernel[offset][None, :] * shifted * matched[:, None]
    return result

def group_step(context, pieces):
    memory, last_seg = context
    values, deltas, log_rates, b_rows, c_rows, segments = pieces
    cumulative = jnp.cumsum(log_rates, axis=0)
    places = jnp.arange(values.shape[0], dtype=jnp.int32)
    linked = (places[:, None] >= places[None, :]) & (segments[:, None] == segments[None, :])
    linked3 = linked[:, :, None]
    spread = jnp.where(linked3, cumulative[:, None, :] - cumulative[None, :, :], 0.0)
    decays = jnp.where(linked3, jnp.exp(spread), 0.0)
    scores = jnp.dot(c_rows, b_rows.T, precision=highest, preferred_element_type=jnp.float32)
    mixing = scores[:, :, None] * decays * deltas[None, :, :]
    inside = jnp.einsum('ijh,jhp->ihp', mixing, values, precision=highest)
    living = (segments == last_seg).astype(values.dtype)
    leading = jnp.exp(cumulative) * living[:, None]
    carried = jnp.einsum('in,hnp->ihp', c_rows, memory, precision=highest) * leading[:, :, None]
    tail_seg = segments[-1]
    ending = cumulative[-1]
    tail_in = jnp.exp(ending[None, :] - cumulative) * (segments == tail_seg).astype(values.dtype)[:, None] * deltas
    retain = jnp.exp(ending) * (tail_seg == last_seg).astype(values.dtype)
    update = jnp.einsum('jh,jn,jhp->hnp', tail_in, b_rows, values, precision=highest)
    return ((memory * retain[:, None, None] + update, tail_seg), inside + carried)

def mixer(z_part, x_part, bc_part, dt_raw, conv_x, conv_bx, conv_bc, conv_bbc, dt_bias, a_log, d_skip, segments, block):
    length = x_part.shape[0]
    head_count = dt_raw.shape[1]
    head_size = x_part.shape[1] // head_count
    blocks = length // block
    conv_out = jax.nn.silu(causal_conv(x_part, conv_x, conv_bx, segments))
    bc_out = jax.nn.silu(causal_conv(bc_part, conv_bc, conv_bbc, segments))
    state_size = bc_out.shape[1] // 2
    deltas = jax.nn.softplus(dt_raw + dt_bias[None, :])
    log_rates = deltas * (-jnp.exp(a_log))[None, :]
    pieces = (conv_out.reshape(blocks, block, head_count, head_size), deltas.reshape(blocks, block, head_count), log_rates.reshape(blocks, block, head_count), bc_out[:, :state_size].reshape(blocks, block, state_size), bc_out[:, state_size:].reshape(blocks, block, state_size), segments.reshape(blocks, block))
    initial = (jnp.zeros((head_count, state_size, head_size), jnp.float32), jnp.array(-1, dtype=jnp.int32))
    final_carry, outputs = lax.scan(jax.checkpoint(group_step), initial, pieces)
    outputs = outputs.reshape(length, head_count, head_size) + d_skip[None, :, None] * conv_out.reshape(length, head_count, head_size)
    return outputs.reshape(length, head_count * head_size) * jax.nn.silu(z_part)

def bin_forward(params, tokens, segments):
    pre_gain, w_z, w_x, w_bc, w_dt, conv_x, conv_bx, conv_bc, conv_bbc, dt_bias, a_log, d_skip, norm_gain, w_out = params
    scaling = lax.rsqrt(lax.optimization_barrier(jnp.mean(tokens * tokens, axis=1, keepdims=True)) + epsilon)
    normed = low(tokens * scaling * pre_gain[None, :])
    z_part = low_back(product(normed, w_z))
    x_part = low_back(product(normed, w_x))
    bc_part = low_back(product(normed, w_bc))
    dt_raw = low_back(product(normed, w_dt))
    gated_out = mixer(z_part, x_part, bc_part, dt_raw, conv_x.reshape(CONV, INNER), conv_bx.reshape(INNER), conv_bc, conv_bbc, dt_bias, a_log, d_skip, segments, BLOCK)
    energy = lax.optimization_barrier(jnp.mean(gated_out * gated_out, axis=1, keepdims=True))
    normal = low(gated_out * lax.rsqrt(energy + epsilon) * norm_gain.reshape(INNER)[None, :])
    return tokens + product(normal, w_out)

def spread_bins(values, order):
    split = values.astype(jnp.float32).reshape(MICRO, N_DP, N_TENSOR, N_DP, PIECE, D)
    picked = jnp.take_along_axis(split, order[:, :, None, :, None, None], axis=3)
    return picked.transpose(0, 3, 2, 1, 4, 5).reshape(MICRO * N_DP, BIN, D)

def gather_back(values, dealing):
    split = values.reshape(MICRO, N_DP, N_TENSOR, N_DP, PIECE, D).transpose(0, 3, 2, 1, 4, 5)
    picked = jnp.take_along_axis(split, dealing[:, :, None, :, None, None], axis=3)
    return picked.reshape(MICRO, ROWS, D)

def reference(tokens, lengths, dealing, cotangent, pre_gain, w_z, w_x, w_bc, w_dt, conv_x, conv_bx, conv_bc, conv_bbc, dt_bias, a_log, d_skip, norm_gain, w_out):
    floats = tuple((p.astype(jnp.float32) for p in (pre_gain, w_z, w_x, w_bc, w_dt, conv_x, conv_bx, conv_bc, conv_bbc, dt_bias, a_log, d_skip, norm_gain, w_out)))
    bin_total = MICRO * BINS
    dealt = dealing.astype(jnp.int32)
    order = jnp.argsort(dealt, axis=2).astype(jnp.int32)
    inputs = spread_bins(tokens, order)
    upstream = spread_bins(cotangent, order)
    segment_table = lax.map(lambda row: segment_ids(row, BIN), lengths.reshape(bin_total, SEQS_BIN).astype(jnp.int32))

    def forward(params, values):

        def one_bin(pair):
            return bin_forward(params, pair[0], pair[1])
        return lax.map(jax.checkpoint(one_bin), (values, segment_table))
    outputs, pullback = jax.vjp(forward, floats, inputs)
    grads, d_inputs = pullback(upstream)
    output = gather_back(outputs.astype(jnp.bfloat16), dealt)
    d_tokens = gather_back(d_inputs.astype(jnp.bfloat16), dealt)
    return (output, d_tokens, grads[0], grads[1], grads[2], grads[3], grads[4], grads[5], grads[6], grads[7], grads[8], grads[9], grads[10], grads[11], grads[12], grads[13])
```

```python
import functools
import math

import jax
import jax.numpy as jnp
from jax import lax
from jax.experimental import pallas as pl
from jax.experimental.pallas import tpu as pltpu
from jax.sharding import PartitionSpec as P

F32 = jnp.float32
BF = jnp.bfloat16
EPS = 1e-05
HALO = 16
CH = 256
LANES = 128
VMEM_LIMIT = 60 * 1024 * 1024


def dot_nn(a, b):
    return lax.dot_general(a, b, (((1,), (0,)), ((), ())), preferred_element_type=F32)


def dot_nt(a, b):
    return lax.dot_general(a, b, (((1,), (1,)), ((), ())), preferred_element_type=F32)


def iota(shape, axis):
    return lax.broadcasted_iota(jnp.int32, shape, axis)


def sigmoid(v):
    return 1.0 / (1.0 + jnp.exp(-v))


def softplus(v):
    return jnp.maximum(v, 0.0) + jnp.log1p(jnp.exp(-jnp.abs(v)))


def bounds_of(lens, m, count):
    total, out = 0, []
    for i in range(count):
        total = total + lens[m, i]
        out.append(total)
    return out


def seg_of(pos, bounds):
    seg = jnp.zeros_like(pos)
    for b in bounds:
        seg = seg + jnp.where(pos >= b, 1, 0)
    return jnp.where(pos < 0, -1, seg)


def prefix_rows(x):
    n = x.shape[0]
    row = iota(x.shape, 0)
    k = 1
    while k < n:
        x = x + jnp.where(row >= k, pltpu.roll(x, k, 0), 0.0)
        k *= 2
    return x


def suffix_rows(x):
    n = x.shape[0]
    row = iota(x.shape, 0)
    k = 1
    while k < n:
        x = x + jnp.where(row < n - k, pltpu.roll(x, n - k, 0), 0.0)
        k *= 2
    return x


def expand(v, first, heads, size):
    rows = v.shape[0]
    per = LANES // size
    lane = iota((rows, LANES), 1)
    cols = []
    for j in range(heads // per):
        h = first + j * per
        block = jnp.broadcast_to(v[:, h : h + 1], (rows, LANES))
        for k in range(1, per):
            block = jnp.where(
                lane >= k * size, jnp.broadcast_to(v[:, h + k : h + k + 1], (rows, LANES)), block
            )
        cols.append(block)
    return jnp.concatenate(cols, axis=1) if len(cols) > 1 else cols[0]


def reducer(first, size, width):
    head = first + iota((width, LANES), 0) // size
    return (head == iota((width, LANES), 1)).astype(BF)


def head_sums(prod, ones):
    high = prod.astype(BF)
    low = (prod - high.astype(F32)).astype(BF)
    return dot_nn(high, ones) + dot_nn(low, ones)


def tap_masks(bounds, pos0, rows, taps):
    pos = pos0 + iota((rows, LANES), 0)
    here = seg_of(pos, bounds)
    return [None] + [
        (seg_of(pos - d, bounds) == here).astype(F32) for d in range(1, taps)
    ]


def wide(mask, width):
    return jnp.concatenate([mask] * (width // LANES), axis=1)


def conv(ext, kernel, bias, masks, taps):
    rows, width = ext.shape[0] - HALO, ext.shape[1]
    total = bias + kernel[taps - 1 : taps] * ext[HALO:]
    for d in range(1, taps):
        total = total + kernel[taps - 1 - d : taps - d] * (
            ext[HALO - d : HALO - d + rows] * wide(masks[d], width)
        )
    return total


def conv_back(ext, dpre, kernel, masks, taps):
    rows, width = dpre.shape
    zeros = jnp.zeros((HALO, width), F32)
    d_ext = None
    d_kernel = []
    for d in range(taps):
        part = dpre if d == 0 else dpre * wide(masks[d], width)
        d_kernel.append(jnp.sum(part * ext[HALO - d : HALO - d + rows], axis=0, keepdims=True))
        padded = jnp.concatenate([zeros, part], axis=0) * kernel[taps - 1 - d : taps - d]
        if d:
            padded = pltpu.roll(padded, rows + HALO - d, 0)
        d_ext = padded if d_ext is None else d_ext + padded
    return d_ext, d_kernel[::-1]


def first_kernel(
    dims, lens, pos0_ref, u, hu, gain, wx, wbc, wdt, kx, bx, kbc, bbc, dtb, alog,
    o_norm, o_xr, o_bcr, o_dt, o_cum, o_xc, o_xh, o_bc, o_s, o_dec,
):
    heads, size, state, taps, seqs = dims
    m = pl.program_id(0)
    rows = u.shape[1]
    inner = wx.shape[1]
    pos0 = pos0_ref[0]
    bounds = bounds_of(lens, m, seqs)

    def norm(v):
        v = v.astype(F32)
        q = lax.rsqrt(jnp.mean(v * v, axis=1, keepdims=True) + EPS)
        return (v * q * gain[...]).astype(BF)

    main = norm(u[0])
    nrm = jnp.concatenate([norm(hu[0]), main], axis=0)
    o_norm[0] = nrm
    dtr = dot_nn(main, wdt[...])
    o_dt[0] = dtr
    delta = softplus(dtr + dtb[...])
    cum = prefix_rows(delta * (-jnp.exp(alog[...])))
    o_cum[0] = cum
    end = cum[rows - 1 : rows]
    tail_seg = seg_of(pos0 + rows - 1, bounds)
    last_seg = seg_of(pos0 - 1, bounds)
    here = seg_of(pos0 + iota((rows, LANES), 0), bounds)
    weight = jnp.exp(end - cum) * (here == tail_seg).astype(F32)
    keep = jnp.exp(jnp.broadcast_to(end, (8, LANES))) * jnp.where(tail_seg == last_seg, 1.0, 0.0)
    masks = tap_masks(bounds, pos0, rows, taps)
    bcr = dot_nn(nrm, wbc[...])
    o_bcr[0] = bcr.astype(BF)
    pre = conv(bcr, kbc[...], bbc[...], masks, taps)
    bc = (pre * sigmoid(pre)).astype(BF)
    o_bc[0] = bc
    bt = bc[:, :state].astype(F32).T.astype(BF)
    per = CH // size
    for c in range(inner // CH):
        at = slice(c * CH, (c + 1) * CH)
        xr = dot_nn(nrm, wx[:, at])
        o_xr[0, :, at] = xr.astype(BF)
        pre = conv(xr, kx[:, at], bx[:, at], masks, taps)
        xc = pre * sigmoid(pre)
        o_xc[0, :, at] = xc.astype(BF)
        xh = (xc * expand(delta, c * per, per, size)).astype(BF)
        o_xh[0, :, at] = xh
        xt = (xh.astype(F32) * expand(weight, c * per, per, size)).astype(BF)
        o_s[0, :, at] = dot_nn(bt, xt)
        o_dec[0, :, at] = expand(keep, c * per, per, size)


def to_slots(out, total):
    if len(out.shape) == 2:
        out[...] = total[...].astype(BF)
        return
    n_dp, n_t, rb, cb = out.shape
    for i in range(n_dp):
        for j in range(n_t):
            out[i, j] = total[i * rb : (i + 1) * rb, j * cb : (j + 1) * cb].astype(BF)


def decay_block(col, row):
    return jnp.exp(jnp.minimum(col - row, 0.0))


def second_kernel(
    dims, lens, pos0_ref, nrm, cum_ref, xc_ref, xh_ref, bc_ref, hin, u, g, wz, wo, ngain, dskip,
    o_out, o_dz, o_dy, o_rd, o_ds, o_dn, o_dwo, o_dwz, o_dgain, o_dskip,
    ynos, zs, gated_s, weighted_s, normal_s, dwo_s, dwz_s,
):
    heads, size, state, taps, seqs = dims
    m = pl.program_id(0)
    rows = u.shape[1]
    inner = wz.shape[1]
    pos0 = pos0_ref[0]
    bounds = bounds_of(lens, m, seqs)
    last_seg = seg_of(pos0 - 1, bounds)
    here = seg_of(pos0 + iota((rows, LANES), 0), bounds)
    cum = cum_ref[0]
    cum_t = cum.T
    lead = jnp.exp(cum) * (here == last_seg).astype(F32)
    t_at, s_at = iota((rows, rows), 0), iota((rows, rows), 1)
    linked = (t_at >= s_at) & (seg_of(pos0 + t_at, bounds) == seg_of(pos0 + s_at, bounds))
    bmat, cmat = bc_ref[0, :, :state], bc_ref[0, :, state:]
    scores = jnp.where(linked, dot_nt(cmat, bmat), 0.0)
    nmain = nrm[0, HALO:, :]
    per = CH // size
    pair = LANES // size
    lane = iota((rows, LANES), 1)
    energy = jnp.zeros((rows, LANES), F32)
    for c in range(inner // CH):
        at = slice(c * CH, (c + 1) * CH)
        blocks = []
        for j in range(per // pair):
            xp = xh_ref[0, :, c * CH + j * LANES : c * CH + (j + 1) * LANES]
            block = None
            for k in range(pair):
                h = c * per + j * pair + k
                mix = (scores * decay_block(cum[:, h : h + 1], cum_t[h : h + 1, :])).astype(BF)
                part = dot_nn(mix, xp)
                block = part if block is None else jnp.where(lane >= k * size, part, block)
            blocks.append(block)
        intra = jnp.concatenate(blocks, axis=1)
        inter = dot_nn(cmat, hin[0, :, at]) * expand(lead, c * per, per, size)
        yn = intra + inter
        ynos[:, at] = yn
        z = dot_nn(nmain, wz[:, at])
        zs[:, at] = z
        y = yn + dskip[:, at] * xc_ref[0, :, at].astype(F32)
        gated = y * (z * sigmoid(z))
        gated_s[:, at] = gated
        for j in range(CH // LANES):
            piece = gated[:, j * LANES : (j + 1) * LANES]
            energy = energy + piece * piece
    rinv = lax.rsqrt(jnp.sum(energy, axis=1, keepdims=True) / inner + EPS)
    gmat = g[0]
    inner_dot = jnp.zeros((rows, LANES), F32)
    dgain = []
    for c in range(inner // CH):
        at = slice(c * CH, (c + 1) * CH)
        gated = gated_s[:, at]
        normal_s[:, at] = (gated * rinv * ngain[:, at]).astype(BF)
        d_normal = dot_nn(gmat, wo[:, at])
        weighted = d_normal * ngain[:, at]
        weighted_s[:, at] = weighted
        dgain.append(jnp.sum(d_normal * gated * rinv, axis=0, keepdims=True))
        prod = weighted * gated
        for j in range(CH // LANES):
            inner_dot = inner_dot + prod[:, j * LANES : (j + 1) * LANES]
    o_out[0] = (u[0].astype(F32) + dot_nt(normal_s[...], wo[...])).astype(BF)
    slope = rinv * rinv * rinv * (jnp.sum(inner_dot, axis=1, keepdims=True) / inner)
    g_t = gmat.astype(F32).T.astype(BF)
    n_t = nmain.astype(F32).T.astype(BF)
    c_t = cmat.astype(F32).T.astype(BF)

    @pl.when(m == 0)
    def _():
        dwo_s[...] = jnp.zeros_like(dwo_s)
        dwz_s[...] = jnp.zeros_like(dwz_s)
        o_dgain[...] = jnp.zeros_like(o_dgain)
        o_dskip[...] = jnp.zeros_like(o_dskip)

    rd = jnp.zeros((rows, LANES), F32)
    dn = jnp.zeros((rows, wz.shape[0]), F32)
    for c in range(inner // CH):
        at = slice(c * CH, (c + 1) * CH)
        gated = gated_s[:, at]
        d_gated = rinv * weighted_s[:, at] - gated * slope
        z = zs[:, at]
        sg = sigmoid(z)
        yn = ynos[:, at]
        xc = xc_ref[0, :, at].astype(F32)
        y = yn + dskip[:, at] * xc
        dy = d_gated * (z * sg)
        dz = (d_gated * y * (sg * (1.0 + z * (1.0 - sg)))).astype(BF)
        o_dz[0, :, at] = dz
        dyb = dy.astype(BF)
        o_dy[0, :, at] = dyb
        dyf = dyb.astype(F32)
        rd = rd + head_sums(dyf * yn, reducer(c * per, size, CH))
        o_dskip[0:1, at] += jnp.sum(dyf * xc, axis=0, keepdims=True)
        o_dgain[0:1, at] += dgain[c]
        o_ds[0, :, at] = dot_nn(c_t, (dyf * expand(lead, c * per, per, size)).astype(BF))
        dwo_s[:, at] += dot_nn(g_t, normal_s[:, at])
        dwz_s[:, at] += dot_nn(n_t, dz)
        dn = dn + dot_nt(dz, wz[:, at])
    o_rd[0] = rd
    o_dn[0] = dn

    @pl.when(m == pl.num_programs(0) - 1)
    def _():
        to_slots(o_dwo, dwo_s)
        to_slots(o_dwz, dwz_s)


def third_kernel(
    dims, lens, pos0_ref, nrm, dtr_ref, cum_ref, xr_ref, bcr_ref, xh_ref, bc_ref, hin, s_ref, dec,
    dso, dy_ref, rd_ref, dnz, wx, wbc, wdt, kx, bx, kbc, bbc, dtb, alog, dskip,
    o_dn, o_dwx, o_dwbc, o_dwdt, o_dkx, o_dkbc, o_ddt,
    dwx_s,
):
    heads, size, state, taps, seqs = dims
    m = pl.program_id(0)
    rows = dtr_ref.shape[1]
    inner = wx.shape[1]
    pos0 = pos0_ref[0]
    bounds = bounds_of(lens, m, seqs)
    tail_seg = seg_of(pos0 + rows - 1, bounds)
    last_seg = seg_of(pos0 - 1, bounds)
    here = seg_of(pos0 + iota((rows, LANES), 0), bounds)
    cum = cum_ref[0]
    cum_t = cum.T
    end = cum[rows - 1 : rows]
    lead = jnp.exp(cum) * (here == last_seg).astype(F32)
    weight = jnp.exp(end - cum) * (here == tail_seg).astype(F32)
    v = dtr_ref[0] + dtb[...]
    delta = softplus(v)
    sg_dt = sigmoid(v)
    s_at, t_at = iota((rows, rows), 0), iota((rows, rows), 1)
    linked = (t_at >= s_at) & (seg_of(pos0 + t_at, bounds) == seg_of(pos0 + s_at, bounds))
    bmat, cmat = bc_ref[0, :, :state], bc_ref[0, :, state:]
    scores = jnp.where(linked, dot_nt(bmat, cmat), 0.0)
    masks = tap_masks(bounds, pos0, rows, taps)
    per = CH // size
    pair = LANES // size
    lane = iota((rows, LANES), 1)

    @pl.when(m == 0)
    def _():
        dwx_s[...] = jnp.zeros_like(dwx_s)
        o_dwbc[...] = jnp.zeros_like(o_dwbc)
        o_dwdt[...] = jnp.zeros_like(o_dwdt)
        o_dkx[...] = jnp.zeros_like(o_dkx)
        o_dkbc[...] = jnp.zeros_like(o_dkbc)
        o_ddt[...] = jnp.zeros_like(o_ddt)

    n_t = nrm[0].astype(F32).T.astype(BF)
    d_scores = jnp.zeros((rows, rows), F32)
    col = jnp.zeros((rows, LANES), F32)
    last = jnp.zeros((8, LANES), F32)
    d_b = jnp.zeros((rows, state), F32)
    d_c = jnp.zeros((rows, state), F32)
    dn = jnp.zeros((rows + HALO, wx.shape[0]), F32)
    for c in range(inner // CH):
        at = slice(c * CH, (c + 1) * CH)
        blocks = []
        for j in range(per // pair):
            span = slice(c * CH + j * LANES, c * CH + (j + 1) * LANES)
            xp, dyp = xh_ref[0, :, span], dy_ref[0, :, span]
            block = None
            for k in range(pair):
                h = c * per + j * pair + k
                fall = decay_block(cum_t[h : h + 1, :], cum[:, h : h + 1])
                mix = (scores * fall).astype(BF)
                part = dot_nn(mix, dyp)
                block = part if block is None else jnp.where(lane >= k * size, part, block)
                mine = (lane >= k * size) & (lane < (k + 1) * size)
                d_scores = d_scores + dot_nt(jnp.where(mine, xp, 0), dyp) * fall
            blocks.append(block)
        intra = jnp.concatenate(blocks, axis=1)
        wide_w = expand(weight, c * per, per, size)
        xh = xh_ref[0, :, at]
        xhf = xh.astype(F32)
        dso_c = dso[0, :, at]
        dxh = intra + dot_nn(bmat, dso_c) * wide_w
        col = col + head_sums(xhf * dxh, reducer(c * per, size, CH))
        d_b = d_b + dot_nt((xhf * wide_w).astype(BF), dso_c)
        dyf = dy_ref[0, :, at].astype(F32)
        h_c = hin[0, :, at]
        d_c = d_c + dot_nt((dyf * expand(lead, c * per, per, size)).astype(BF), h_c)
        s_out = s_ref[0, :, at] + dec[0, 0:1, at] * h_c.astype(F32)
        both = jnp.sum(dso_c.astype(F32) * s_out, axis=0, keepdims=True)
        last = last + head_sums(jnp.broadcast_to(both, (8, CH)), reducer(c * per, size, CH))
        d_xc = dxh * expand(delta, c * per, per, size) + dskip[:, at] * dyf
        ext = xr_ref[0, :, at].astype(F32)
        pre = conv(ext, kx[:, at], bx[:, at], masks, taps)
        sg = sigmoid(pre)
        dpre = d_xc * (sg * (1.0 + pre * (1.0 - sg)))
        d_ext, d_kernel = conv_back(ext, dpre, kx[:, at], masks, taps)
        for k in range(taps):
            o_dkx[k : k + 1, at] += d_kernel[k]
        o_dkx[taps : taps + 1, at] += jnp.sum(dpre, axis=0, keepdims=True)
        dxr = d_ext.astype(BF)
        dn = dn + dot_nt(dxr, wx[:, at])
        dwx_s[:, at] += dot_nn(n_t, dxr)
    d_scores = jnp.where(linked, d_scores, 0.0)
    d_b = d_b + dot_nn(d_scores.astype(BF), cmat)
    d_c = d_c + dot_nn(d_scores.T.astype(BF), bmat)
    d_bc = jnp.concatenate([d_b, d_c], axis=1)
    ext = bcr_ref[0].astype(F32)
    pre = conv(ext, kbc[...], bbc[...], masks, taps)
    sg = sigmoid(pre)
    dpre = d_bc * (sg * (1.0 + pre * (1.0 - sg)))
    d_ext, d_kernel = conv_back(ext, dpre, kbc[...], masks, taps)
    for k in range(taps):
        o_dkbc[k : k + 1, :] += d_kernel[k]
    o_dkbc[taps : taps + 1, :] += jnp.sum(dpre, axis=0, keepdims=True)
    dbcr = d_ext.astype(BF)
    dn = dn + dot_nt(dbcr, wbc[...])
    o_dwbc[...] += dot_nn(n_t, dbcr)
    row = iota((rows, LANES), 0)
    d_cum = rd_ref[0] - col + jnp.where(row == rows - 1, jnp.broadcast_to(last[0:1], (rows, LANES)), 0.0)
    d_rate = suffix_rows(d_cum)
    rate_of = -jnp.exp(alog[...])
    ratio = jnp.where(delta > 1e-30, sg_dt / jnp.maximum(delta, 1e-30), 1.0)
    d_dt = col * ratio + d_rate * rate_of * sg_dt
    o_ddt[0:1, :] += jnp.sum(d_dt, axis=0, keepdims=True)
    o_ddt[1:2, :] += jnp.sum(d_rate * delta * rate_of, axis=0, keepdims=True)
    d_dtb = d_dt.astype(BF)
    o_dwdt[...] += dot_nn(n_t[:, HALO:], d_dtb)
    o_dn[0, :HALO, :] = dn[:HALO]
    o_dn[0, HALO:, :] = dn[HALO:] + dot_nt(d_dtb, wdt[...]) + dnz[0]

    @pl.when(m == pl.num_programs(0) - 1)
    def _():
        to_slots(o_dwx, dwx_s)


MESH = pl.DeviceIdType.MESH


class Place:
    def __init__(self, n_dp, n_t):
        self.n_dp, self.n_t, self.n_p = n_dp, n_t, n_dp // 2
        self.dp, self.t = lax.axis_index("dp"), lax.axis_index("tensor")
        self.plane, self.core = lax.div(self.dp, 2), lax.rem(self.dp, 2)
        self.sibling = (self.plane * 2 + 1 - self.core, self.t)

    def up(self, s):
        return lax.rem(self.t + s, self.n_t)

    def down(self, s):
        return lax.rem(self.t + self.n_t - s, self.n_t)

    def plane_up(self, s):
        return lax.rem(self.plane + s, self.n_p)

    def plane_down(self, s):
        return lax.rem(self.plane + self.n_p - s, self.n_p)

    def dp_up(self, s):
        return lax.rem(self.dp + s, self.n_dp)

    def dp_down(self, s):
        return lax.rem(self.dp + self.n_dp - s, self.n_dp)

    def barrier(self):
        sem = pltpu.get_barrier_semaphore()
        for s in range(1, self.n_t):
            pl.semaphore_signal(sem, inc=1, device_id=(self.dp, self.up(s)), device_id_type=MESH)
        for s in range(1, self.n_dp):
            pl.semaphore_signal(sem, inc=1, device_id=(self.dp_up(s), self.t), device_id_type=MESH)
        pl.semaphore_wait(sem, self.n_t + self.n_dp - 2)


def remote(src, dst, send, recv, to):
    return pltpu.make_async_remote_copy(
        src_ref=src, dst_ref=dst, send_sem=send, recv_sem=recv, device_id=to, device_id_type=MESH
    )


def dma(count):
    return pltpu.SemaphoreType.DMA((count,))


class Gather:
    def __init__(self, place, src, out, sems):
        self.p, self.src, self.out = place, src, out
        self.local, self.zs, self.zr, self.ps, self.pr, self.cs, self.cr = sems
        self.sent = []
        self.block = src.shape

    @staticmethod
    def scratch(n_dp, n_t):
        n_p = n_dp // 2
        return [dma(1), dma(n_t - 1), dma(n_t - 1), dma(n_p - 1), dma(n_p - 1), dma(n_p), dma(n_p)]

    def slot(self, dp, t):
        if len(self.out.shape) == 4:
            return self.out.at[dp, t]
        rb, cb = self.block
        return self.out.at[
            pl.ds(pl.multiple_of(dp * rb, rb), rb), pl.ds(pl.multiple_of(t * cb, cb), cb)
        ]

    def band(self, dp):
        if len(self.out.shape) == 4:
            return self.out.at[dp]
        rb = self.block[0]
        return self.out.at[pl.ds(pl.multiple_of(dp * rb, rb), rb), :]

    def go(self, src, dst, send, recv, to):
        copy = remote(src, dst, send, recv, to)
        copy.start()
        self.sent.append(copy)

    def start_z(self):
        p = self.p
        mine = self.slot(p.dp, p.t)
        for s in range(1, p.n_t):
            self.go(self.src, mine, self.zs.at[s - 1], self.zr.at[s - 1], (p.dp, p.up(s)))
        self.own = pltpu.make_async_copy(self.src, mine, self.local.at[0])
        self.own.start()

    def start_p(self):
        p = self.p
        self.own.wait()
        for s in range(1, p.n_t):
            view = self.slot(p.dp, p.down(s))
            remote(view, view, self.zs.at[s - 1], self.zr.at[s - 1], (p.dp, p.t)).wait_recv()
        view = self.band(p.dp)
        for s in range(1, p.n_p):
            to = (p.plane_up(s) * 2 + p.core, p.t)
            self.go(view, view, self.ps.at[s - 1], self.pr.at[s - 1], to)
        self.go(view, view, self.cs.at[0], self.cr.at[0], p.sibling)

    def start_c(self):
        p = self.p
        for s in range(1, p.n_p):
            view = self.band(p.plane_down(s) * 2 + p.core)
            remote(view, view, self.ps.at[s - 1], self.pr.at[s - 1], p.sibling).wait_recv()
            self.go(view, view, self.cs.at[s], self.cr.at[s], p.sibling)

    def finish(self):
        p = self.p
        for s in range(p.n_p):
            view = self.band(p.plane_down(s) * 2 + 1 - p.core)
            remote(view, view, self.cs.at[s], self.cr.at[s], p.sibling).wait_recv()
        for copy in self.sent:
            copy.wait_send()


class Scatter:
    def __init__(self, place, src, out, bufs):
        self.p, self.src, self.out = place, src, out
        self.cb, self.pb, self.zb, self.zo = bufs[:4]
        self.cs, self.cr, self.ps, self.pr, self.zs, self.zr = bufs[4:]
        self.sent = []

    @staticmethod
    def scratch(n_dp, n_t, block, dtype):
        n_p = n_dp // 2
        return [
            pltpu.VMEM((n_p, n_t) + block, dtype), pltpu.VMEM((n_p - 1, n_t) + block, dtype),
            pltpu.VMEM((n_t - 1,) + block, dtype), pltpu.VMEM((n_t,) + block, dtype),
            dma(n_p), dma(n_p), dma(n_p - 1), dma(n_p - 1), dma(n_t - 1), dma(n_t - 1),
        ]

    go = Gather.go

    def start_c(self):
        p = self.p
        for s in list(range(1, p.n_p)) + [0]:
            q = p.plane_up(s)
            self.go(
                self.src.at[q * 2 + 1 - p.core], self.cb.at[q], self.cs.at[s], self.cr.at[s],
                p.sibling,
            )

    def start_p(self):
        p = self.p
        for s in list(range(1, p.n_p)) + [0]:
            q = p.plane_up(s)
            view = self.cb.at[q]
            remote(view, view, self.cs.at[s], self.cr.at[s], p.sibling).wait_recv()

            @pl.loop(0, p.n_t)
            def _(t):
                own = self.src[q * 2 + p.core, t].astype(F32)
                self.cb[q, t] = (own + self.cb[q, t].astype(F32)).astype(self.cb.dtype)

            if s:
                self.go(
                    view, self.pb.at[s - 1], self.ps.at[s - 1], self.pr.at[s - 1],
                    (q * 2 + p.core, p.t),
                )

    def start_z(self):
        p = self.p
        for s in range(1, p.n_p):
            view = self.pb.at[s - 1]
            remote(view, view, self.ps.at[s - 1], self.pr.at[s - 1], p.sibling).wait_recv()
        for s in list(range(1, p.n_t)) + [0]:
            t = p.up(s)
            total = self.cb[p.plane, t].astype(F32)
            for k in range(p.n_p - 1):
                total = total + self.pb[k, t].astype(F32)
            if s:
                self.zo[s] = total.astype(self.zo.dtype)
                self.go(
                    self.zo.at[s], self.zb.at[s - 1], self.zs.at[s - 1], self.zr.at[s - 1],
                    (p.dp, t),
                )
            else:
                self.out[...] = total

    def finish(self):
        p = self.p
        total = self.out[...]
        for s in range(1, p.n_t):
            view = self.zb.at[s - 1]
            remote(view, view, self.zs.at[s - 1], self.zr.at[s - 1], p.sibling).wait_recv()
            total = total + self.zb[s - 1].astype(F32)
        self.out[...] = total
        for copy in self.sent:
            copy.wait_send()


class Deal:
    def __init__(self, place, order, src, out, bufs):
        self.p, self.order, self.src, self.out = place, order, src, out
        self.buf, self.ss, self.rs = bufs
        self.sent = []

    @staticmethod
    def scratch(n_dp, shape):
        micro, _, piece, width = shape
        return [pltpu.VMEM((n_dp, micro, piece, width), BF), dma(n_dp - 1), dma(n_dp - 1)]

    go = Gather.go

    def start(self):
        p = self.p
        micro = self.src.shape[0]
        for s in list(range(1, p.n_dp)) + [0]:
            r = p.dp_up(s)
            for m in range(micro):
                rows = self.src[m, self.order[m, r]]
                if s:
                    self.buf[s, m] = rows
                else:
                    self.out[m, p.dp] = rows
            if s:
                self.go(
                    self.buf.at[s], self.out.at[:, p.dp], self.ss.at[s - 1], self.rs.at[s - 1],
                    (r, p.t),
                )

    def finish(self):
        p = self.p
        for s in range(1, p.n_dp):
            view = self.out.at[:, p.dp_down(s)]
            remote(view, view, self.ss.at[s - 1], self.rs.at[s - 1], p.sibling).wait_recv()
        for copy in self.sent:
            copy.wait_send()


class Undeal:
    def __init__(self, place, deal, src, out, bufs):
        self.p, self.deal, self.src, self.out = place, deal, src, out
        self.buf, self.ss, self.rs = bufs
        self.sent = []

    @staticmethod
    def scratch(n_dp, shape):
        return [pltpu.VMEM(shape, BF), dma(n_dp - 1), dma(n_dp - 1)]

    go = Gather.go

    def start(self):
        p = self.p
        for s in range(1, p.n_dp):
            r = p.dp_up(s)
            self.go(
                self.src.at[:, r], self.buf.at[:, p.dp], self.ss.at[s - 1], self.rs.at[s - 1],
                (r, p.t),
            )
        for m in range(self.src.shape[0]):
            self.buf[m, p.dp] = self.src[m, p.dp]

    def finish(self):
        p = self.p
        for s in range(1, p.n_dp):
            view = self.buf.at[:, p.dp_down(s)]
            remote(view, view, self.ss.at[s - 1], self.rs.at[s - 1], p.sibling).wait_recv()
        for m in range(self.src.shape[0]):
            for k in range(p.n_dp):
                self.out[m, k] = self.buf[m, self.deal[m, k]]
        for copy in self.sent:
            copy.wait_send()


PARTS = 3


class Chain:
    def __init__(self, place, step, terms, keep, out, bufs):
        self.p, self.step, self.terms, self.keep, self.out = place, step, terms, keep, out
        self.buf, self.ss, self.rs = bufs
        self.first = place.t == (0 if step > 0 else place.n_t - 1)
        self.last = place.t == (place.n_t - 1 if step > 0 else 0)
        self.count = terms.shape[0] * PARTS

    @staticmethod
    def scratch(shape):
        count = shape[0] * PARTS
        return [pltpu.VMEM((count, shape[1], shape[2] // PARTS), BF), dma(count), dma(count)]

    def copy(self, j):
        m, width = j // PARTS, self.terms.shape[2] // PARTS
        at = slice((j % PARTS) * width, (j % PARTS + 1) * width)
        to = (self.p.dp, jnp.clip(self.p.t + self.step, 0, self.p.n_t - 1))
        view = self.out.at[m, :, at]
        return m, at, remote(self.buf.at[j], view, self.ss.at[j], self.rs.at[j], to)

    def run(self, j):
        m, at, copy = self.copy(j)

        @pl.when(jnp.logical_not(self.first))
        def _():
            copy.wait_recv()

        @pl.when(self.first)
        def _():
            self.out[m, :, at] = jnp.zeros(self.buf.shape[1:], BF)

        @pl.when(jnp.logical_not(self.last))
        def _():
            self.buf[j] = (
                self.terms[m, :, at] + self.keep[m, 0:1, at] * self.out[m, :, at].astype(F32)
            ).astype(BF)
            copy.start()

    def finish(self):
        for j in range(self.count):
            copy = self.copy(j)[2]

            @pl.when(jnp.logical_not(self.last))
            def _():
                copy.wait_send()


class Halo:
    def __init__(self, place, step, out, sems):
        self.p, self.step, self.out = place, step, out
        self.ss, self.rs = sems
        self.first = place.t == (0 if step > 0 else place.n_t - 1)
        self.last = place.t == (place.n_t - 1 if step > 0 else 0)

    def start(self, src):
        to = (self.p.dp, jnp.clip(self.p.t + self.step, 0, self.p.n_t - 1))
        spare = self.out.shape[1] - src.shape[1]
        view = self.out.at[:, spare:, :] if spare else self.out
        self.copy = remote(src, view, self.ss.at[0], self.rs.at[0], to)
        if spare:
            self.out[:, :spare, :] = jnp.zeros(
                (self.out.shape[0], spare, self.out.shape[2]), self.out.dtype
            )

        @pl.when(jnp.logical_not(self.last))
        def _():
            self.copy.start()

        @pl.when(self.first)
        def _():
            self.out[:, spare:, :] = jnp.zeros(src.shape, self.out.dtype)

    def finish(self):
        @pl.when(jnp.logical_not(self.first))
        def _():
            self.copy.wait_recv()

        @pl.when(jnp.logical_not(self.last))
        def _():
            self.copy.wait_send()


def take(refs, counts):
    out, at = [], 0
    for count in counts:
        out.append(refs[at : at + count])
        at += count
    return out


def enter_kernel(n_dp, n_t, order, tokens, wx, wbc, pack, u, halo, o_wx, o_wbc, o_pack, *scratch):
    p = Place(n_dp, n_t)
    parts = take(scratch, (7, 7, 7, 3, 2))
    p.barrier()
    deal = Deal(p, order, tokens, u, parts[3])
    gathers = [
        Gather(p, a, b, c) for a, b, c in zip((pack, wbc, wx), (o_pack, o_wbc, o_wx), parts[:3])
    ]
    for gather in gathers:
        gather.start_z()
    deal.start()
    for gather in gathers:
        gather.start_p()
    deal.finish()
    tail = Halo(p, 1, halo, parts[4])
    piece = u.shape[2]
    tail.start(u.at[:, n_dp - 1, max(piece - HALO, 0) : piece, :])
    for gather in gathers:
        gather.start_c()
    for gather in gathers:
        gather.finish()
    tail.finish()


def ahead_kernel(n_dp, n_t, order, cot, wz, wo, terms, keep, g, hin, o_wz, o_wo, *scratch):
    p = Place(n_dp, n_t)
    parts = take(scratch, (7, 7, 3, 3))
    p.barrier()
    deal = Deal(p, order, cot, g, parts[2])
    chain = Chain(p, 1, terms, keep, hin, parts[3])
    gathers = [Gather(p, a, b, c) for a, b, c in zip((wz, wo), (o_wz, o_wo), parts[:2])]
    for gather in gathers:
        gather.start_z()
    half = chain.count // 2
    for j in range(half):
        chain.run(j)
    deal.start()
    gathers[0].start_p()
    for j in range(half, chain.count):
        chain.run(j)
    gathers[1].start_p()
    for gather in gathers:
        gather.start_c()
    for gather in gathers:
        gather.finish()
    deal.finish()
    chain.finish()


def behind_kernel(n_dp, n_t, deal, rows, dwz, dwo, terms, keep, out, dso, o_z, o_o, *scratch):
    p = Place(n_dp, n_t)
    parts = take(scratch, (10, 10, 3, 3))
    p.barrier()
    undeal = Undeal(p, deal, rows, out, parts[2])
    chain = Chain(p, -1, terms, keep, dso, parts[3])
    scatters = [Scatter(p, a, b, c) for a, b, c in zip((dwo, dwz), (o_o, o_z), parts[:2])]
    for scatter in scatters:
        scatter.start_c()
    third = chain.count // 3
    for j in range(third):
        chain.run(j)
    scatters[0].start_p()
    undeal.start()
    for j in range(third, 2 * third):
        chain.run(j)
    scatters[1].start_p()
    for j in range(2 * third, chain.count):
        chain.run(j)
    for scatter in scatters:
        scatter.start_z()
    for scatter in scatters:
        scatter.finish()
    undeal.finish()
    chain.finish()


def leave_kernel(n_dp, n_t, deal, rows, dwx, dwbc, pack, out, o_x, o_bc, o_pack, *scratch):
    p = Place(n_dp, n_t)
    parts = take(scratch, (10, 10, 10, 3))
    p.barrier()
    undeal = Undeal(p, deal, rows, out, parts[3])
    scatters = [
        Scatter(p, a, b, c)
        for a, b, c in zip((pack, dwbc, dwx), (o_pack, o_bc, o_x), parts[:3])
    ]
    for scatter in scatters:
        scatter.start_c()
    undeal.start()
    for scatter in scatters:
        scatter.start_p()
    for scatter in scatters:
        scatter.start_z()
    for scatter in scatters:
        scatter.finish()
    undeal.finish()


IN_VMEM = pl.BlockSpec(memory_space=pltpu.VMEM)
IN_PLACE = pl.BlockSpec(memory_space=pl.ANY)


def talk(kernel, n_dp, n_t, number, operands, spaces, outs, scratch):
    return pl.pallas_call(
        functools.partial(kernel, n_dp, n_t),
        in_specs=spaces,
        out_specs=[space for _, _, space in outs],
        out_shape=[jax.ShapeDtypeStruct(s, d) for s, d, _ in outs],
        scratch_shapes=scratch,
        compiler_params=pltpu.CompilerParams(
            collective_id=number, has_side_effects=True, vmem_limit_bytes=VMEM_LIMIT
        ),
    )(*operands)


def by_micro(shape):
    return pl.BlockSpec((1,) + tuple(shape[1:]), lambda m: (m,) + (0,) * (len(shape) - 1))


def whole(shape):
    return pl.BlockSpec(tuple(shape), lambda m: (0,) * len(shape))


SCALARS = pl.BlockSpec(memory_space=pltpu.SMEM)


def call(kernel, dims, micro, scalars, per_micro, shared, outs, scratch):
    in_specs = (
        [SCALARS] * len(scalars)
        + [by_micro(x.shape) for x in per_micro]
        + [whole(x.shape) for x in shared]
    )
    out_specs = [by_micro(s) if split else whole(s) for s, _, split in outs]
    return pl.pallas_call(
        functools.partial(kernel, dims),
        grid=(micro,),
        in_specs=in_specs,
        out_specs=out_specs,
        out_shape=[jax.ShapeDtypeStruct(s, d) for s, d, _ in outs],
        scratch_shapes=[pltpu.VMEM(s, d) for s, d in scratch],
        compiler_params=pltpu.CompilerParams(vmem_limit_bytes=VMEM_LIMIT),
    )(*scalars, *per_micro, *shared)


def pad_lanes(x, width=LANES):
    return jnp.pad(x, [(0, 0)] * (x.ndim - 1) + [(0, width - x.shape[-1])])


def pad_rows(x, rows=8):
    return jnp.pad(x, [(0, rows - x.shape[0])] + [(0, 0)] * (x.ndim - 1))


def local(
    tokens, lengths, dealing, cotangent, pre_gain, w_z, w_x, w_bc, w_dt, conv_x, conv_bx, conv_bc,
    conv_bbc, dt_bias, a_log, d_skip, norm_gain, w_out,
):
    micro, rows, width = tokens.shape
    n_dp, n_t = lax.axis_size("dp"), lax.axis_size("tensor")
    place = lax.axis_index("tensor")
    piece = rows // n_dp
    deal = dealing[:, 0, :]
    lens = lengths[:, 0, :]
    pos0 = (place * rows).reshape(1).astype(jnp.int32)

    slots = jnp.arange(n_dp, dtype=jnp.int32)
    deal = deal.astype(jnp.int32)
    order = jnp.sum(
        jnp.where(deal[:, None, :] == slots[None, :, None], slots[None, None, :], 0), axis=2
    )
    pieces = (micro, n_dp, piece, width)
    rb, cb = w_x.shape
    aligned = rb % 16 == 0 and cb % LANES == 0
    inner = cb * n_t
    taps, per_t, size_d = conv_x.shape
    heads, size = per_t * n_t, size_d * n_dp
    state = conv_bc.shape[1] * n_dp * n_t // 2
    seqs = lens.shape[1]
    dims = (heads, size, state, taps, seqs)

    lengths_of = [
        (taps + 2) * per_t * size_d, pre_gain.shape[0], (taps + 1) * conv_bc.shape[1],
        w_dt.shape[0] * per_t, 3 * per_t,
    ]
    used = sum(lengths_of)
    total = -(-used // 1024) * 1024
    stacked = jnp.concatenate([conv_x, conv_bx[None], norm_gain[None]], axis=0)
    bc_small = jnp.concatenate([conv_bc, conv_bbc[None]], axis=0)
    pack = jnp.concatenate(
        [
            stacked.reshape(-1).astype(F32), pre_gain.astype(F32), bc_small.reshape(-1).astype(F32),
            w_dt.reshape(-1).astype(F32), dt_bias, a_log, d_skip, jnp.zeros((total - used,), F32),
        ]
    ).reshape(total // LANES, LANES)
    starts = [0]
    for length in lengths_of:
        starts.append(starts[-1] + length)

    def gathered(shape, dtype):
        full_shape = (shape[0] * n_dp, shape[1] * n_t)
        return (full_shape if aligned else (n_dp, n_t) + shape, dtype, IN_PLACE)

    def joined(w):
        return w if aligned else w.transpose(0, 2, 1, 3).reshape(rb * n_dp, inner)

    u, halo, wx, wbc, packs = talk(
        enter_kernel, n_dp, n_t, 1, (order, tokens.reshape(pieces), w_x, w_bc, pack),
        [SCALARS, IN_VMEM, IN_PLACE, IN_PLACE, IN_PLACE],
        [
            (pieces, BF, IN_VMEM), ((micro, HALO, width), BF, IN_VMEM), gathered((rb, cb), BF),
            ((n_dp, n_t) + w_bc.shape, BF, IN_PLACE), ((n_dp, n_t) + pack.shape, F32, IN_PLACE),
        ],
        Gather.scratch(n_dp, n_t) * 3 + Deal.scratch(n_dp, pieces) + [dma(1), dma(1)],
    )
    u = u.reshape(micro, rows, width)
    wx = joined(wx)
    wbc = wbc.reshape(width, 2 * state)
    packs = packs.reshape(n_dp, n_t, total)
    cut = [packs[:, :, a:b] for a, b in zip(starts, starts[1:])]
    stacked = cut[0].reshape(n_dp, n_t, taps + 2, per_t, size_d).transpose(2, 1, 3, 0, 4)
    stacked = stacked.reshape(taps + 2, inner)
    gain = cut[1].reshape(1, width)
    bc_small = cut[2].reshape(n_dp * n_t, taps + 1, -1).transpose(1, 0, 2).reshape(taps + 1, 2 * state)
    wdt_p = pad_lanes(
        cut[3].reshape(n_dp, n_t, rb, per_t).transpose(0, 2, 1, 3).reshape(width, heads).astype(BF)
    )
    heads_f = cut[4][0].reshape(n_t, 3, per_t).transpose(1, 0, 2).reshape(3, heads)
    kx, bx, ngain = pad_rows(stacked[:taps]), stacked[taps : taps + 1], stacked[taps + 1 :]
    kbc_p, bbc = pad_rows(bc_small[:taps]), bc_small[taps:]
    dtb, alog = pad_lanes(heads_f[0:1]), pad_lanes(heads_f[1:2])
    dskip = jnp.repeat(heads_f[2], size)[None, :]

    nrm, xr, bcr, dtr, cum, xc, xh, bc, s_loc, dec = call(
        first_kernel, dims, micro, (lens, pos0), (u, halo),
        (gain, wx, wbc, wdt_p, kx, bx, kbc_p, bbc, dtb, alog),
        [
            ((micro, rows + HALO, width), BF, True),
            ((micro, rows + HALO, inner), BF, True),
            ((micro, rows + HALO, 2 * state), BF, True),
            ((micro, rows, LANES), F32, True),
            ((micro, rows, LANES), F32, True),
            ((micro, rows, inner), BF, True),
            ((micro, rows, inner), BF, True),
            ((micro, rows, 2 * state), BF, True),
            ((micro, state, inner), F32, True),
            ((micro, 8, inner), F32, True),
        ],
        [],
    )
    states = (micro, state, inner)
    g, hin, wz, wo = talk(
        ahead_kernel, n_dp, n_t, 2, (order, cotangent.reshape(pieces), w_z, w_out.T, s_loc, dec),
        [SCALARS, IN_VMEM, IN_PLACE, IN_PLACE, IN_VMEM, IN_VMEM],
        [
            (pieces, BF, IN_VMEM), (states, BF, IN_VMEM), gathered((rb, cb), BF),
            gathered((rb, cb), BF),
        ],
        Gather.scratch(n_dp, n_t) * 2 + Deal.scratch(n_dp, pieces) + Chain.scratch(states),
    )
    g = g.reshape(micro, rows, width)
    wz, wo = joined(wz), joined(wo)
    slot_shape = (n_dp, n_t, rb, cb)
    grad_shape = slot_shape if aligned else (width, inner)

    def parted(w):
        return w if aligned else w.reshape(n_dp, rb, n_t, cb).transpose(0, 2, 1, 3)

    out_rows, dz, dy, rd, ds_loc, dnz, dwo, dwz, dgain, ddskip = call(
        second_kernel, dims, micro, (lens, pos0), (nrm, cum, xc, xh, bc, hin, u, g),
        (wz, wo, ngain, dskip),
        [
            ((micro, rows, width), BF, True),
            ((micro, rows, inner), BF, True),
            ((micro, rows, inner), BF, True),
            ((micro, rows, LANES), F32, True),
            ((micro, state, inner), F32, True),
            ((micro, rows, width), F32, True),
            (grad_shape, BF, False),
            (grad_shape, BF, False),
            ((8, inner), F32, False),
            ((8, inner), F32, False),
        ],
        [
            ((rows, inner), F32), ((rows, inner), F32), ((rows, inner), F32), ((rows, inner), F32),
            ((rows, inner), BF), ((width, inner), F32), ((width, inner), F32),
        ],
    )
    output, dso, sum_z, sum_o = talk(
        behind_kernel, n_dp, n_t, 3,
        (deal, out_rows.reshape(pieces), parted(dwz), parted(dwo), ds_loc, dec),
        [SCALARS] + [IN_VMEM] * 5,
        [
            (pieces, BF, IN_VMEM), (states, BF, IN_VMEM), ((rb, cb), F32, IN_VMEM),
            ((rb, cb), F32, IN_VMEM),
        ],
        Scatter.scratch(n_dp, n_t, (rb, cb), BF) * 2 + Undeal.scratch(n_dp, pieces)
        + Chain.scratch(states),
    )
    dn, dwx, dwbc, dwdt, dkx, dkbc, ddt = call(
        third_kernel, dims, micro, (lens, pos0),
        (nrm, dtr, cum, xr, bcr, xh, bc, hin, s_loc, dec, dso, dy, rd, dnz),
        (wx, wbc, wdt_p, kx, bx, kbc_p, bbc, dtb, alog, dskip),
        [
            ((micro, rows + HALO, width), F32, True),
            (grad_shape, BF, False),
            ((width, 2 * state), F32, False),
            ((width, LANES), F32, False),
            ((8, inner), F32, False),
            ((8, 2 * state), F32, False),
            ((8, LANES), F32, False),
        ],
        [((width, inner), F32)],
    )
    back = [(i + 1, i) for i in range(n_t - 1)]
    spill = lax.ppermute(dn[:, :HALO, :], "tensor", back)
    dn = dn[:, HALO:, :] + jnp.pad(spill, [(0, 0), (rows - HALO, 0), (0, 0)])
    uf = u.astype(F32)
    q = lax.rsqrt(jnp.mean(uf * uf, axis=2, keepdims=True) + EPS)
    f = dn * gain[None]
    d_u = q * f - uf * (q * q * q) * (jnp.sum(f * uf, axis=2, keepdims=True) / width)
    d_pre = jnp.sum(dn * uf * q, axis=(0, 1))
    dtok_rows = (g.astype(F32) + d_u).astype(BF)

    stacked_g = jnp.concatenate([dkx[: taps + 1], dgain[0:1]], axis=0)
    stacked_g = stacked_g.reshape(taps + 2, n_t, per_t, n_dp, size_d).transpose(3, 1, 0, 2, 4)
    bc_g = dkbc[: taps + 1].reshape(taps + 1, n_dp, n_t, -1).transpose(1, 2, 0, 3)
    dt_g = dwdt[:, :heads].reshape(n_dp, rb, n_t, per_t).transpose(0, 2, 1, 3)
    heads_g = jnp.stack([ddt[0, :heads], ddt[1, :heads], ddskip[0].reshape(heads, size).sum(1)])
    heads_g = heads_g.reshape(3, n_t, per_t).transpose(1, 0, 2)
    heads_g = jnp.broadcast_to(heads_g[None], (n_dp,) + heads_g.shape)
    pack_g = jnp.concatenate(
        [
            stacked_g.reshape(n_dp, n_t, -1), d_pre.reshape(n_dp, n_t, -1),
            bc_g.reshape(n_dp, n_t, -1), dt_g.reshape(n_dp, n_t, -1),
            heads_g.reshape(n_dp, n_t, -1), jnp.zeros((n_dp, n_t, total - used), F32),
        ],
        axis=2,
    ).reshape((n_dp, n_t) + pack.shape)
    d_tokens, sum_x, d_wbc, sums = talk(
        leave_kernel, n_dp, n_t, 4,
        (
            deal, dtok_rows.reshape(pieces), parted(dwx),
            dwbc.astype(BF).reshape((n_dp, n_t) + w_bc.shape), pack_g,
        ),
        [SCALARS] + [IN_VMEM] * 4,
        [
            (pieces, BF, IN_VMEM), ((rb, cb), F32, IN_VMEM), (w_bc.shape, F32, IN_VMEM),
            (pack.shape, F32, IN_VMEM),
        ],
        Scatter.scratch(n_dp, n_t, pack.shape, F32) + Scatter.scratch(n_dp, n_t, w_bc.shape, BF)
        + Scatter.scratch(n_dp, n_t, (rb, cb), BF) + Undeal.scratch(n_dp, pieces),
    )
    sums = sums.reshape(total)
    got = [sums[a:b] for a, b in zip(starts, starts[1:])]
    got_stacked = got[0].reshape(taps + 2, per_t, size_d)
    got_bc = got[2].reshape(taps + 1, -1)
    got_heads = got[4].reshape(3, per_t)
    return (
        output.reshape(tokens.shape), d_tokens.reshape(tokens.shape), got[1], sum_z, sum_x, d_wbc,
        got[3].reshape(rb, per_t), got_stacked[:taps], got_stacked[taps], got_bc[:taps],
        got_bc[taps], got_heads[0], got_heads[1], got_heads[2], got_stacked[taps + 1], sum_o.T,
    )


def solution(mesh):
    both = ("dp", "tensor")
    in_specs = (
        P(None, both, None), P(None, "dp", None), P(None, "dp", None), P(None, both, None), P(both),
        P("dp", "tensor"), P("dp", "tensor"), P(both, None), P("dp", "tensor"),
        P(None, "tensor", "dp"), P("tensor", "dp"), P(None, both), P(both), P("tensor"),
        P("tensor"), P("tensor"), P("tensor", "dp"), P("tensor", "dp"),
    )
    out_specs = (
        P(None, both, None), P(None, both, None), P(both), P("dp", "tensor"), P("dp", "tensor"),
        P(both, None), P("dp", "tensor"), P(None, "tensor", "dp"), P("tensor", "dp"), P(None, both),
        P(both), P("tensor"), P("tensor"), P("tensor"), P("tensor", "dp"), P("tensor", "dp"),
    )
    return jax.shard_map(local, mesh=mesh, in_specs=in_specs, out_specs=out_specs, check_vma=False)
```

```python
import functools
import math

import jax
import jax.numpy as jnp
from jax import lax
from jax.experimental import pallas as pl
from jax.experimental.pallas import tpu as pltpu
from jax.sharding import PartitionSpec as P

F32 = jnp.float32
BF = jnp.bfloat16
EPS = 1e-05
HALO = 16
CH = 256
LANES = 128
VMEM_LIMIT = 60 * 1024 * 1024
MEGA_LIMIT = 63 * 1024 * 1024


def dot_nn(a, b):
    return lax.dot_general(a, b, (((1,), (0,)), ((), ())), preferred_element_type=F32)


def dot_nt(a, b):
    return lax.dot_general(a, b, (((1,), (1,)), ((), ())), preferred_element_type=F32)


def iota(shape, axis):
    return lax.broadcasted_iota(jnp.int32, shape, axis)


def sigmoid(v):
    return 1.0 / (1.0 + jnp.exp(-v))


def softplus(v):
    return jnp.maximum(v, 0.0) + jnp.log1p(jnp.exp(-jnp.abs(v)))


def bounds_of(lens, m, count):
    total, out = 0, []
    for i in range(count):
        total = total + lens[m, i]
        out.append(total)
    return out


def seg_of(pos, bounds):
    seg = jnp.zeros_like(pos)
    for b in bounds:
        seg = seg + jnp.where(pos >= b, 1, 0)
    return jnp.where(pos < 0, -1, seg)


def prefix_rows(x):
    n = x.shape[0]
    row = iota(x.shape, 0)
    k = 1
    while k < n:
        x = x + jnp.where(row >= k, pltpu.roll(x, k, 0), 0.0)
        k *= 2
    return x


def suffix_rows(x):
    n = x.shape[0]
    row = iota(x.shape, 0)
    k = 1
    while k < n:
        x = x + jnp.where(row < n - k, pltpu.roll(x, n - k, 0), 0.0)
        k *= 2
    return x


def expand(v, first, heads, size):
    rows = v.shape[0]
    per = LANES // size
    lane = iota((rows, LANES), 1)
    cols = []
    for j in range(heads // per):
        h = first + j * per
        block = jnp.broadcast_to(v[:, h : h + 1], (rows, LANES))
        for k in range(1, per):
            block = jnp.where(
                lane >= k * size, jnp.broadcast_to(v[:, h + k : h + k + 1], (rows, LANES)), block
            )
        cols.append(block)
    return jnp.concatenate(cols, axis=1) if len(cols) > 1 else cols[0]


def reducer(first, size, width):
    head = first + iota((width, LANES), 0) // size
    return (head == iota((width, LANES), 1)).astype(BF)


def head_sums(prod, ones):
    high = prod.astype(BF)
    low = (prod - high.astype(F32)).astype(BF)
    return dot_nn(high, ones) + dot_nn(low, ones)


def reach(bounds, pos0, rows, taps):
    pos = pos0 + iota((rows, LANES), 0)
    here = seg_of(pos, bounds)
    far = jnp.zeros((rows, LANES), F32)
    for d in range(1, taps):
        far = far + (seg_of(pos - d, bounds) == here).astype(F32)
    return far


def wide(mask, width):
    return jnp.concatenate([mask] * (width // LANES), axis=1)


def near(part, far, d):
    return part if d == 0 else jnp.where(wide(far, part.shape[1]) >= d, part, 0.0)


def conv(ext, kernel, bias, far, taps):
    rows = ext.shape[0] - HALO
    total = bias + kernel[taps - 1 : taps] * ext[HALO:]
    for d in range(1, taps):
        total = total + kernel[taps - 1 - d : taps - d] * near(
            ext[HALO - d : HALO - d + rows], far, d
        )
    return total


def conv_back(ext, dpre, kernel, far, taps):
    rows, width = dpre.shape
    zeros = jnp.zeros((HALO, width), F32)
    d_ext = None
    d_kernel = []
    for d in range(taps):
        part = near(dpre, far, d)
        d_kernel.append(jnp.sum(part * ext[HALO - d : HALO - d + rows], axis=0, keepdims=True))
        padded = jnp.concatenate([zeros, part], axis=0) * kernel[taps - 1 - d : taps - d]
        if d:
            padded = pltpu.roll(padded, rows + HALO - d, 0)
        d_ext = padded if d_ext is None else d_ext + padded
    return d_ext, d_kernel[::-1]


def first_kernel(
    dims, lens, pos0_ref, u, hu, gain, wx, wbc, wdt, kx, bx, kbc, bbc, dtb, alog,
    o_norm, o_xr, o_bcr, o_dt, o_cum, o_xc, o_xh, o_bc, o_s, o_dec,
):
    heads, size, state, taps, seqs = dims
    m = pl.program_id(0)
    rows = u.shape[1]
    inner = wx.shape[1]
    pos0 = pos0_ref[0]
    bounds = bounds_of(lens, m, seqs)

    def norm(v):
        v = v.astype(F32)
        q = lax.rsqrt(jnp.mean(v * v, axis=1, keepdims=True) + EPS)
        return (v * q * gain[...]).astype(BF)

    main = norm(u[0])
    nrm = jnp.concatenate([norm(hu[0]), main], axis=0)
    o_norm[0] = nrm
    dtr = dot_nn(main, wdt[...])
    o_dt[0] = dtr
    delta = softplus(dtr + dtb[...])
    cum = prefix_rows(delta * (-jnp.exp(alog[...])))
    o_cum[0] = cum
    end = cum[rows - 1 : rows]
    tail_seg = seg_of(pos0 + rows - 1, bounds)
    last_seg = seg_of(pos0 - 1, bounds)
    here = seg_of(pos0 + iota((rows, LANES), 0), bounds)
    weight = jnp.exp(end - cum) * (here == tail_seg).astype(F32)
    keep = jnp.exp(jnp.broadcast_to(end, (8, LANES))) * jnp.where(tail_seg == last_seg, 1.0, 0.0)
    far = reach(bounds, pos0, rows, taps)
    bcr = dot_nn(nrm, wbc[...])
    o_bcr[0] = bcr.astype(BF)
    pre = conv(bcr, kbc[...], bbc[...], far, taps)
    bc = (pre * sigmoid(pre)).astype(BF)
    o_bc[0] = bc
    bt = bc[:, :state].astype(F32).T.astype(BF)
    per = CH // size
    for c in range(inner // CH):
        at = slice(c * CH, (c + 1) * CH)
        xr = dot_nn(nrm, wx[:, at])
        o_xr[0, :, at] = xr.astype(BF)
        pre = conv(xr, kx[:, at], bx[:, at], far, taps)
        xc = pre * sigmoid(pre)
        o_xc[0, :, at] = xc.astype(BF)
        xh = (xc * expand(delta, c * per, per, size)).astype(BF)
        o_xh[0, :, at] = xh
        xt = (xh.astype(F32) * expand(weight, c * per, per, size)).astype(BF)
        o_s[0, :, at] = dot_nn(bt, xt)
        o_dec[0, :, at] = expand(keep, c * per, per, size)


def to_slots(out, total):
    if len(out.shape) == 2:
        out[...] = total[...].astype(BF)
        return
    n_dp, n_t, rb, cb = out.shape
    for i in range(n_dp):
        for j in range(n_t):
            out[i, j] = total[i * rb : (i + 1) * rb, j * cb : (j + 1) * cb].astype(BF)


def decay_block(col, row):
    return jnp.exp(jnp.minimum(col - row, 0.0))


def second_kernel(
    dims, lens, pos0_ref, nrm, cum_ref, xc_ref, xh_ref, bc_ref, hin, u, g, wz, wo, ngain, dskip,
    o_out, o_dz, o_dy, o_rd, o_ds, o_dn, o_dwo, o_dwz, o_dgain, o_dskip,
    ynos, zs, gated_s, weighted_s, normal_s, dwo_s, dwz_s,
):
    heads, size, state, taps, seqs = dims
    m = pl.program_id(0)
    rows = u.shape[1]
    inner = wz.shape[1]
    pos0 = pos0_ref[0]
    bounds = bounds_of(lens, m, seqs)
    last_seg = seg_of(pos0 - 1, bounds)
    here = seg_of(pos0 + iota((rows, LANES), 0), bounds)
    cum = cum_ref[0]
    cum_t = cum.T
    lead = jnp.exp(cum) * (here == last_seg).astype(F32)
    t_at, s_at = iota((rows, rows), 0), iota((rows, rows), 1)
    linked = (t_at >= s_at) & (seg_of(pos0 + t_at, bounds) == seg_of(pos0 + s_at, bounds))
    bmat, cmat = bc_ref[0, :, :state], bc_ref[0, :, state:]
    scores = jnp.where(linked, dot_nt(cmat, bmat), 0.0)
    nmain = nrm[0, HALO:, :]
    per = CH // size
    pair = LANES // size
    lane = iota((rows, LANES), 1)
    energy = jnp.zeros((rows, LANES), F32)
    for c in range(inner // CH):
        at = slice(c * CH, (c + 1) * CH)
        blocks = []
        for j in range(per // pair):
            xp = xh_ref[0, :, c * CH + j * LANES : c * CH + (j + 1) * LANES]
            block = None
            for k in range(pair):
                h = c * per + j * pair + k
                mix = (scores * decay_block(cum[:, h : h + 1], cum_t[h : h + 1, :])).astype(BF)
                part = dot_nn(mix, xp)
                block = part if block is None else jnp.where(lane >= k * size, part, block)
            blocks.append(block)
        intra = jnp.concatenate(blocks, axis=1)
        inter = dot_nn(cmat, hin[0, :, at]) * expand(lead, c * per, per, size)
        yn = intra + inter
        ynos[:, at] = yn
        z = dot_nn(nmain, wz[:, at])
        zs[:, at] = z
        y = yn + dskip[:, at] * xc_ref[0, :, at].astype(F32)
        gated = y * (z * sigmoid(z))
        gated_s[:, at] = gated
        for j in range(CH // LANES):
            piece = gated[:, j * LANES : (j + 1) * LANES]
            energy = energy + piece * piece
    rinv = lax.rsqrt(jnp.sum(energy, axis=1, keepdims=True) / inner + EPS)
    gmat = g[0]
    inner_dot = jnp.zeros((rows, LANES), F32)
    dgain = []
    for c in range(inner // CH):
        at = slice(c * CH, (c + 1) * CH)
        gated = gated_s[:, at]
        normal_s[:, at] = (gated * rinv * ngain[:, at]).astype(BF)
        d_normal = dot_nn(gmat, wo[:, at])
        weighted = d_normal * ngain[:, at]
        weighted_s[:, at] = weighted
        dgain.append(jnp.sum(d_normal * gated * rinv, axis=0, keepdims=True))
        prod = weighted * gated
        for j in range(CH // LANES):
            inner_dot = inner_dot + prod[:, j * LANES : (j + 1) * LANES]
    o_out[0] = (u[0].astype(F32) + dot_nt(normal_s[...], wo[...])).astype(BF)
    slope = rinv * rinv * rinv * (jnp.sum(inner_dot, axis=1, keepdims=True) / inner)
    g_t = gmat.astype(F32).T.astype(BF)
    n_t = nmain.astype(F32).T.astype(BF)
    c_t = cmat.astype(F32).T.astype(BF)

    @pl.when(m == 0)
    def _():
        dwo_s[...] = jnp.zeros_like(dwo_s)
        dwz_s[...] = jnp.zeros_like(dwz_s)
        o_dgain[...] = jnp.zeros_like(o_dgain)
        o_dskip[...] = jnp.zeros_like(o_dskip)

    rd = jnp.zeros((rows, LANES), F32)
    dn = jnp.zeros((rows, wz.shape[0]), F32)
    for c in range(inner // CH):
        at = slice(c * CH, (c + 1) * CH)
        gated = gated_s[:, at]
        d_gated = rinv * weighted_s[:, at] - gated * slope
        z = zs[:, at]
        sg = sigmoid(z)
        yn = ynos[:, at]
        xc = xc_ref[0, :, at].astype(F32)
        y = yn + dskip[:, at] * xc
        dy = d_gated * (z * sg)
        dz = (d_gated * y * (sg * (1.0 + z * (1.0 - sg)))).astype(BF)
        o_dz[0, :, at] = dz
        dyb = dy.astype(BF)
        o_dy[0, :, at] = dyb
        dyf = dyb.astype(F32)
        rd = rd + head_sums(dyf * yn, reducer(c * per, size, CH))
        o_dskip[0:1, at] += jnp.sum(dyf * xc, axis=0, keepdims=True)
        o_dgain[0:1, at] += dgain[c]
        o_ds[0, :, at] = dot_nn(c_t, (dyf * expand(lead, c * per, per, size)).astype(BF))
        dwo_s[:, at] += dot_nn(g_t, normal_s[:, at])
        dwz_s[:, at] += dot_nn(n_t, dz)
        dn = dn + dot_nt(dz, wz[:, at])
    o_rd[0] = rd
    o_dn[0] = dn

    @pl.when(m == pl.num_programs(0) - 1)
    def _():
        to_slots(o_dwo, dwo_s)
        to_slots(o_dwz, dwz_s)


def third_kernel(
    dims, lens, pos0_ref, nrm, dtr_ref, cum_ref, xr_ref, bcr_ref, xh_ref, bc_ref, hin, s_ref, dec,
    dso, dy_ref, rd_ref, dnz, wx, wbc, wdt, kx, bx, kbc, bbc, dtb, alog, dskip,
    o_dn, o_dwx, o_dwbc, o_dwdt, o_dkx, o_dkbc, o_ddt,
    dwx_s,
):
    heads, size, state, taps, seqs = dims
    m = pl.program_id(0)
    rows = dtr_ref.shape[1]
    inner = wx.shape[1]
    pos0 = pos0_ref[0]
    bounds = bounds_of(lens, m, seqs)
    tail_seg = seg_of(pos0 + rows - 1, bounds)
    last_seg = seg_of(pos0 - 1, bounds)
    here = seg_of(pos0 + iota((rows, LANES), 0), bounds)
    cum = cum_ref[0]
    cum_t = cum.T
    end = cum[rows - 1 : rows]
    lead = jnp.exp(cum) * (here == last_seg).astype(F32)
    weight = jnp.exp(end - cum) * (here == tail_seg).astype(F32)
    v = dtr_ref[0] + dtb[...]
    delta = softplus(v)
    sg_dt = sigmoid(v)
    s_at, t_at = iota((rows, rows), 0), iota((rows, rows), 1)
    linked = (t_at >= s_at) & (seg_of(pos0 + t_at, bounds) == seg_of(pos0 + s_at, bounds))
    bmat, cmat = bc_ref[0, :, :state], bc_ref[0, :, state:]
    scores = jnp.where(linked, dot_nt(bmat, cmat), 0.0)
    far = reach(bounds, pos0, rows, taps)
    per = CH // size
    pair = LANES // size
    lane = iota((rows, LANES), 1)

    @pl.when(m == 0)
    def _():
        dwx_s[...] = jnp.zeros_like(dwx_s)
        o_dwbc[...] = jnp.zeros_like(o_dwbc)
        o_dwdt[...] = jnp.zeros_like(o_dwdt)
        o_dkx[...] = jnp.zeros_like(o_dkx)
        o_dkbc[...] = jnp.zeros_like(o_dkbc)
        o_ddt[...] = jnp.zeros_like(o_ddt)

    n_t = nrm[0].astype(F32).T.astype(BF)
    d_scores = jnp.zeros((rows, rows), F32)
    col = jnp.zeros((rows, LANES), F32)
    last = jnp.zeros((8, LANES), F32)
    d_b = jnp.zeros((rows, state), F32)
    d_c = jnp.zeros((rows, state), F32)
    dn = jnp.zeros((rows + HALO, wx.shape[0]), F32)
    for c in range(inner // CH):
        at = slice(c * CH, (c + 1) * CH)
        blocks = []
        for j in range(per // pair):
            span = slice(c * CH + j * LANES, c * CH + (j + 1) * LANES)
            xp, dyp = xh_ref[0, :, span], dy_ref[0, :, span]
            block = None
            for k in range(pair):
                h = c * per + j * pair + k
                fall = decay_block(cum_t[h : h + 1, :], cum[:, h : h + 1])
                mix = (scores * fall).astype(BF)
                part = dot_nn(mix, dyp)
                block = part if block is None else jnp.where(lane >= k * size, part, block)
                mine = (lane >= k * size) & (lane < (k + 1) * size)
                d_scores = d_scores + dot_nt(jnp.where(mine, xp, 0), dyp) * fall
            blocks.append(block)
        intra = jnp.concatenate(blocks, axis=1)
        wide_w = expand(weight, c * per, per, size)
        xh = xh_ref[0, :, at]
        xhf = xh.astype(F32)
        dso_c = dso[0, :, at]
        passed = dot_nn(bmat, dso_c)
        dxh = intra + passed * wide_w
        xt = (xhf * wide_w).astype(BF)
        col = col + head_sums(xhf * intra + xt.astype(F32) * passed, reducer(c * per, size, CH))
        d_b = d_b + dot_nt(xt, dso_c)
        dyf = dy_ref[0, :, at].astype(F32)
        h_c = hin[0, :, at]
        d_c = d_c + dot_nt((dyf * expand(lead, c * per, per, size)).astype(BF), h_c)
        s_out = s_ref[0, :, at] + dec[0, 0:1, at] * h_c.astype(F32)
        both = jnp.sum(dso_c.astype(F32) * s_out, axis=0, keepdims=True)
        last = last + head_sums(jnp.broadcast_to(both, (8, CH)), reducer(c * per, size, CH))
        d_xc = dxh * expand(delta, c * per, per, size) + dskip[:, at] * dyf
        ext = xr_ref[0, :, at].astype(F32)
        pre = conv(ext, kx[:, at], bx[:, at], far, taps)
        sg = sigmoid(pre)
        dpre = d_xc * (sg * (1.0 + pre * (1.0 - sg)))
        d_ext, d_kernel = conv_back(ext, dpre, kx[:, at], far, taps)
        for k in range(taps):
            o_dkx[k : k + 1, at] += d_kernel[k]
        o_dkx[taps : taps + 1, at] += jnp.sum(dpre, axis=0, keepdims=True)
        dxr = d_ext.astype(BF)
        dn = dn + dot_nt(dxr, wx[:, at])
        dwx_s[:, at] += dot_nn(n_t, dxr)
    d_scores = jnp.where(linked, d_scores, 0.0)
    d_b = d_b + dot_nn(d_scores.astype(BF), cmat)
    d_c = d_c + dot_nn(d_scores.T.astype(BF), bmat)
    d_bc = jnp.concatenate([d_b, d_c], axis=1)
    ext = bcr_ref[0].astype(F32)
    pre = conv(ext, kbc[...], bbc[...], far, taps)
    sg = sigmoid(pre)
    dpre = d_bc * (sg * (1.0 + pre * (1.0 - sg)))
    d_ext, d_kernel = conv_back(ext, dpre, kbc[...], far, taps)
    for k in range(taps):
        o_dkbc[k : k + 1, :] += d_kernel[k]
    o_dkbc[taps : taps + 1, :] += jnp.sum(dpre, axis=0, keepdims=True)
    dbcr = d_ext.astype(BF)
    dn = dn + dot_nt(dbcr, wbc[...])
    o_dwbc[...] += dot_nn(n_t, dbcr)
    row = iota((rows, LANES), 0)
    d_cum = rd_ref[0] - col + jnp.where(row == rows - 1, jnp.broadcast_to(last[0:1], (rows, LANES)), 0.0)
    d_rate = suffix_rows(d_cum)
    rate_of = -jnp.exp(alog[...])
    ratio = jnp.where(delta > 1e-30, sg_dt / jnp.maximum(delta, 1e-30), 1.0)
    d_dt = col * ratio + d_rate * rate_of * sg_dt
    o_ddt[0:1, :] += jnp.sum(d_dt, axis=0, keepdims=True)
    o_ddt[1:2, :] += jnp.sum(d_rate * delta * rate_of, axis=0, keepdims=True)
    d_dtb = d_dt.astype(BF)
    o_dwdt[...] += dot_nn(n_t[:, HALO:], d_dtb)
    o_dn[0, :HALO, :] = dn[:HALO]
    o_dn[0, HALO:, :] = dn[HALO:] + dot_nt(d_dtb, wdt[...]) + dnz[0]

    @pl.when(m == pl.num_programs(0) - 1)
    def _():
        to_slots(o_dwx, dwx_s)


MESH = pl.DeviceIdType.MESH


class Place:
    def __init__(self, n_dp, n_t):
        self.n_dp, self.n_t, self.n_p = n_dp, n_t, n_dp // 2
        self.dp, self.t = lax.axis_index("dp"), lax.axis_index("tensor")
        self.plane, self.core = lax.div(self.dp, 2), lax.rem(self.dp, 2)
        self.sibling = (self.plane * 2 + 1 - self.core, self.t)

    def up(self, s):
        return lax.rem(self.t + s, self.n_t)

    def down(self, s):
        return lax.rem(self.t + self.n_t - s, self.n_t)

    def plane_up(self, s):
        return lax.rem(self.plane + s, self.n_p)

    def plane_down(self, s):
        return lax.rem(self.plane + self.n_p - s, self.n_p)

    def dp_up(self, s):
        return lax.rem(self.dp + s, self.n_dp)

    def dp_down(self, s):
        return lax.rem(self.dp + self.n_dp - s, self.n_dp)

    def barrier(self):
        sem = pltpu.get_barrier_semaphore()
        for s in range(1, self.n_t):
            pl.semaphore_signal(sem, inc=1, device_id=(self.dp, self.up(s)), device_id_type=MESH)
        for s in range(1, self.n_dp):
            pl.semaphore_signal(sem, inc=1, device_id=(self.dp_up(s), self.t), device_id_type=MESH)
        pl.semaphore_wait(sem, self.n_t + self.n_dp - 2)


def remote(src, dst, send, recv, to):
    return pltpu.make_async_remote_copy(
        src_ref=src, dst_ref=dst, send_sem=send, recv_sem=recv, device_id=to, device_id_type=MESH
    )


def dma(count):
    return pltpu.SemaphoreType.DMA((count,))


class Gather:
    def __init__(self, place, src, out, sems):
        self.p, self.src, self.out = place, src, out
        self.local, self.zs, self.zr, self.ps, self.pr, self.cs, self.cr = sems
        self.sent = []
        self.block = src.shape

    @staticmethod
    def scratch(n_dp, n_t):
        n_p = n_dp // 2
        return [dma(1), dma(n_t - 1), dma(n_t - 1), dma(n_p - 1), dma(n_p - 1), dma(n_p), dma(n_p)]

    def slot(self, dp, t):
        if len(self.out.shape) == 4:
            return self.out.at[dp, t]
        rb, cb = self.block
        return self.out.at[
            pl.ds(pl.multiple_of(dp * rb, rb), rb), pl.ds(pl.multiple_of(t * cb, cb), cb)
        ]

    def band(self, dp):
        if len(self.out.shape) == 4:
            return self.out.at[dp]
        rb = self.block[0]
        return self.out.at[pl.ds(pl.multiple_of(dp * rb, rb), rb), :]

    def go(self, src, dst, send, recv, to):
        copy = remote(src, dst, send, recv, to)
        copy.start()
        self.sent.append(copy)

    def start_z(self):
        p = self.p
        mine = self.slot(p.dp, p.t)
        for s in range(1, p.n_t):
            self.go(self.src, mine, self.zs.at[s - 1], self.zr.at[s - 1], (p.dp, p.up(s)))
        self.own = pltpu.make_async_copy(self.src, mine, self.local.at[0])
        self.own.start()

    def start_p(self):
        p = self.p
        self.own.wait()
        for s in range(1, p.n_t):
            view = self.slot(p.dp, p.down(s))
            remote(view, view, self.zs.at[s - 1], self.zr.at[s - 1], (p.dp, p.t)).wait_recv()
        view = self.band(p.dp)
        for s in range(1, p.n_p):
            to = (p.plane_up(s) * 2 + p.core, p.t)
            self.go(view, view, self.ps.at[s - 1], self.pr.at[s - 1], to)
        self.go(view, view, self.cs.at[0], self.cr.at[0], p.sibling)

    def start_c(self):
        p = self.p
        for s in range(1, p.n_p):
            view = self.band(p.plane_down(s) * 2 + p.core)
            remote(view, view, self.ps.at[s - 1], self.pr.at[s - 1], p.sibling).wait_recv()
            self.go(view, view, self.cs.at[s], self.cr.at[s], p.sibling)

    def finish(self):
        p = self.p
        for s in range(p.n_p):
            view = self.band(p.plane_down(s) * 2 + 1 - p.core)
            remote(view, view, self.cs.at[s], self.cr.at[s], p.sibling).wait_recv()
        for copy in self.sent:
            copy.wait_send()


class Scatter:
    def __init__(self, place, src, out, bufs):
        self.p, self.src, self.out = place, src, out
        self.cb, self.pb, self.zb, self.zo = bufs[:4]
        self.cs, self.cr, self.ps, self.pr, self.zs, self.zr = bufs[4:]
        self.sent = []

    @staticmethod
    def scratch(n_dp, n_t, block, dtype):
        n_p = n_dp // 2
        return [
            pltpu.VMEM((n_p, n_t) + block, dtype), pltpu.VMEM((n_p - 1, n_t) + block, dtype),
            pltpu.VMEM((n_t - 1,) + block, dtype), pltpu.VMEM((n_t,) + block, dtype),
            dma(n_p), dma(n_p), dma(n_p - 1), dma(n_p - 1), dma(n_t - 1), dma(n_t - 1),
        ]

    go = Gather.go

    def start_c(self):
        p = self.p
        for s in list(range(1, p.n_p)) + [0]:
            q = p.plane_up(s)
            self.go(
                self.src.at[q * 2 + 1 - p.core], self.cb.at[q], self.cs.at[s], self.cr.at[s],
                p.sibling,
            )

    def start_p(self):
        p = self.p
        for s in list(range(1, p.n_p)) + [0]:
            q = p.plane_up(s)
            view = self.cb.at[q]
            remote(view, view, self.cs.at[s], self.cr.at[s], p.sibling).wait_recv()

            @pl.loop(0, p.n_t)
            def _(t):
                own = self.src[q * 2 + p.core, t].astype(F32)
                self.cb[q, t] = (own + self.cb[q, t].astype(F32)).astype(self.cb.dtype)

            if s:
                self.go(
                    view, self.pb.at[s - 1], self.ps.at[s - 1], self.pr.at[s - 1],
                    (q * 2 + p.core, p.t),
                )

    def start_z(self):
        p = self.p
        for s in range(1, p.n_p):
            view = self.pb.at[s - 1]
            remote(view, view, self.ps.at[s - 1], self.pr.at[s - 1], p.sibling).wait_recv()
        for s in list(range(1, p.n_t)) + [0]:
            t = p.up(s)
            total = self.cb[p.plane, t].astype(F32)
            for k in range(p.n_p - 1):
                total = total + self.pb[k, t].astype(F32)
            if s:
                self.zo[s] = total.astype(self.zo.dtype)
                self.go(
                    self.zo.at[s], self.zb.at[s - 1], self.zs.at[s - 1], self.zr.at[s - 1],
                    (p.dp, t),
                )
            else:
                self.out[...] = total

    def finish(self):
        p = self.p
        total = self.out[...]
        for s in range(1, p.n_t):
            view = self.zb.at[s - 1]
            remote(view, view, self.zs.at[s - 1], self.zr.at[s - 1], p.sibling).wait_recv()
            total = total + self.zb[s - 1].astype(F32)
        self.out[...] = total
        for copy in self.sent:
            copy.wait_send()


class Deal:
    def __init__(self, place, order, src, out, bufs):
        self.p, self.order, self.src, self.out = place, order, src, out
        self.buf, self.ss, self.rs = bufs
        self.sent = []

    @staticmethod
    def scratch(n_dp, shape):
        micro, _, piece, width = shape
        return [pltpu.VMEM((n_dp, micro, piece, width), BF), dma(n_dp - 1), dma(n_dp - 1)]

    go = Gather.go

    def start(self):
        p = self.p
        micro = self.src.shape[0]
        for s in list(range(1, p.n_dp)) + [0]:
            r = p.dp_up(s)
            for m in range(micro):
                rows = self.src[m, self.order[m, r]]
                if s:
                    self.buf[s, m] = rows
                else:
                    self.out[m, p.dp] = rows
            if s:
                self.go(
                    self.buf.at[s], self.out.at[:, p.dp], self.ss.at[s - 1], self.rs.at[s - 1],
                    (r, p.t),
                )

    def finish(self):
        p = self.p
        for s in range(1, p.n_dp):
            view = self.out.at[:, p.dp_down(s)]
            remote(view, view, self.ss.at[s - 1], self.rs.at[s - 1], p.sibling).wait_recv()
        for copy in self.sent:
            copy.wait_send()


class Undeal:
    def __init__(self, place, deal, src, out, bufs):
        self.p, self.deal, self.src, self.out = place, deal, src, out
        self.buf, self.ss, self.rs = bufs
        self.sent = []

    @staticmethod
    def scratch(n_dp, shape):
        return [pltpu.VMEM(shape, BF), dma(n_dp - 1), dma(n_dp - 1)]

    go = Gather.go

    def start(self):
        p = self.p
        for s in range(1, p.n_dp):
            r = p.dp_up(s)
            self.go(
                self.src.at[:, r], self.buf.at[:, p.dp], self.ss.at[s - 1], self.rs.at[s - 1],
                (r, p.t),
            )
        for m in range(self.src.shape[0]):
            self.buf[m, p.dp] = self.src[m, p.dp]

    def finish(self):
        p = self.p
        for s in range(1, p.n_dp):
            view = self.buf.at[:, p.dp_down(s)]
            remote(view, view, self.ss.at[s - 1], self.rs.at[s - 1], p.sibling).wait_recv()
        for m in range(self.src.shape[0]):
            for k in range(p.n_dp):
                self.out[m, k] = self.buf[m, self.deal[m, k]]
        for copy in self.sent:
            copy.wait_send()


PARTS = 3


class Chain:
    def __init__(self, place, step, terms, keep, out, bufs):
        self.p, self.step, self.terms, self.keep, self.out = place, step, terms, keep, out
        self.buf, self.ss, self.rs = bufs
        self.first = place.t == (0 if step > 0 else place.n_t - 1)
        self.last = place.t == (place.n_t - 1 if step > 0 else 0)
        self.count = terms.shape[0] * PARTS

    @staticmethod
    def scratch(shape):
        count = shape[0] * PARTS
        return [pltpu.VMEM((count, shape[1], shape[2] // PARTS), BF), dma(count), dma(count)]

    def copy(self, j):
        m, width = j // PARTS, self.terms.shape[2] // PARTS
        at = slice((j % PARTS) * width, (j % PARTS + 1) * width)
        to = (self.p.dp, jnp.clip(self.p.t + self.step, 0, self.p.n_t - 1))
        view = self.out.at[m, :, at]
        return m, at, remote(self.buf.at[j], view, self.ss.at[j], self.rs.at[j], to)

    def run(self, j):
        m, at, copy = self.copy(j)

        @pl.when(jnp.logical_not(self.first))
        def _():
            copy.wait_recv()

        @pl.when(self.first)
        def _():
            self.out[m, :, at] = jnp.zeros(self.buf.shape[1:], BF)

        @pl.when(jnp.logical_not(self.last))
        def _():
            self.buf[j] = (
                self.terms[m, :, at] + self.keep[m, 0:1, at] * self.out[m, :, at].astype(F32)
            ).astype(BF)
            copy.start()

    def finish(self):
        for j in range(self.count):
            copy = self.copy(j)[2]

            @pl.when(jnp.logical_not(self.last))
            def _():
                copy.wait_send()


class Halo:
    def __init__(self, place, step, out, sems):
        self.p, self.step, self.out = place, step, out
        self.ss, self.rs = sems
        self.first = place.t == (0 if step > 0 else place.n_t - 1)
        self.last = place.t == (place.n_t - 1 if step > 0 else 0)

    def start(self, src):
        to = (self.p.dp, jnp.clip(self.p.t + self.step, 0, self.p.n_t - 1))
        spare = self.out.shape[1] - src.shape[1]
        view = self.out.at[:, spare:, :] if spare else self.out
        self.copy = remote(src, view, self.ss.at[0], self.rs.at[0], to)
        if spare:
            self.out[:, :spare, :] = jnp.zeros(
                (self.out.shape[0], spare, self.out.shape[2]), self.out.dtype
            )

        @pl.when(jnp.logical_not(self.last))
        def _():
            self.copy.start()

        @pl.when(self.first)
        def _():
            self.out[:, spare:, :] = jnp.zeros(src.shape, self.out.dtype)

    def finish(self):
        @pl.when(jnp.logical_not(self.first))
        def _():
            self.copy.wait_recv()

        @pl.when(jnp.logical_not(self.last))
        def _():
            self.copy.wait_send()


def take(refs, counts):
    out, at = [], 0
    for count in counts:
        out.append(refs[at : at + count])
        at += count
    return out


def enter_kernel(n_dp, n_t, order, tokens, wx, wbc, pack, u, halo, o_wx, o_wbc, o_pack, *scratch):
    p = Place(n_dp, n_t)
    parts = take(scratch, (7, 7, 7, 3, 2))
    p.barrier()
    deal = Deal(p, order, tokens, u, parts[3])
    gathers = [
        Gather(p, a, b, c) for a, b, c in zip((pack, wbc, wx), (o_pack, o_wbc, o_wx), parts[:3])
    ]
    for gather in gathers:
        gather.start_z()
    deal.start()
    for gather in gathers:
        gather.start_p()
    deal.finish()
    tail = Halo(p, 1, halo, parts[4])
    piece = u.shape[2]
    tail.start(u.at[:, n_dp - 1, max(piece - HALO, 0) : piece, :])
    for gather in gathers:
        gather.start_c()
    for gather in gathers:
        gather.finish()
    tail.finish()


def ahead_kernel(n_dp, n_t, order, cot, wz, wo, terms, keep, g, hin, o_wz, o_wo, *scratch):
    p = Place(n_dp, n_t)
    parts = take(scratch, (7, 7, 3, 3))
    p.barrier()
    deal = Deal(p, order, cot, g, parts[2])
    chain = Chain(p, 1, terms, keep, hin, parts[3])
    gathers = [Gather(p, a, b, c) for a, b, c in zip((wz, wo), (o_wz, o_wo), parts[:2])]
    for gather in gathers:
        gather.start_z()
    half = chain.count // 2
    for j in range(half):
        chain.run(j)
    deal.start()
    gathers[0].start_p()
    for j in range(half, chain.count):
        chain.run(j)
    gathers[1].start_p()
    for gather in gathers:
        gather.start_c()
    for gather in gathers:
        gather.finish()
    deal.finish()
    chain.finish()


def behind_kernel(n_dp, n_t, deal, rows, dwz, dwo, terms, keep, out, dso, o_z, o_o, *scratch):
    p = Place(n_dp, n_t)
    parts = take(scratch, (10, 10, 3, 3))
    p.barrier()
    undeal = Undeal(p, deal, rows, out, parts[2])
    chain = Chain(p, -1, terms, keep, dso, parts[3])
    scatters = [Scatter(p, a, b, c) for a, b, c in zip((dwo, dwz), (o_o, o_z), parts[:2])]
    for scatter in scatters:
        scatter.start_c()
    third = chain.count // 3
    for j in range(third):
        chain.run(j)
    scatters[0].start_p()
    undeal.start()
    for j in range(third, 2 * third):
        chain.run(j)
    scatters[1].start_p()
    for j in range(2 * third, chain.count):
        chain.run(j)
    for scatter in scatters:
        scatter.start_z()
    for scatter in scatters:
        scatter.finish()
    undeal.finish()
    chain.finish()


def leave_kernel(n_dp, n_t, deal, rows, dwx, dwbc, pack, out, o_x, o_bc, o_pack, *scratch):
    p = Place(n_dp, n_t)
    parts = take(scratch, (10, 10, 10, 3))
    p.barrier()
    undeal = Undeal(p, deal, rows, out, parts[3])
    scatters = [
        Scatter(p, a, b, c)
        for a, b, c in zip((pack, dwbc, dwx), (o_pack, o_bc, o_x), parts[:3])
    ]
    for scatter in scatters:
        scatter.start_c()
    undeal.start()
    for scatter in scatters:
        scatter.start_p()
    for scatter in scatters:
        scatter.start_z()
    for scatter in scatters:
        scatter.finish()
    undeal.finish()


IN_VMEM = pl.BlockSpec(memory_space=pltpu.VMEM)
IN_PLACE = pl.BlockSpec(memory_space=pl.ANY)


def talk(kernel, n_dp, n_t, number, operands, spaces, outs, scratch):
    return pl.pallas_call(
        functools.partial(kernel, n_dp, n_t),
        in_specs=spaces,
        out_specs=[space for _, _, space in outs],
        out_shape=[jax.ShapeDtypeStruct(s, d) for s, d, _ in outs],
        scratch_shapes=scratch,
        compiler_params=pltpu.CompilerParams(
            collective_id=number, has_side_effects=True, vmem_limit_bytes=VMEM_LIMIT
        ),
    )(*operands)


LAG = 2


class Sums:
    def __init__(self, place, src, out, bufs):
        self.p, self.src, self.out = place, src, out
        self.cb, self.pb, self.zb = bufs[:3]
        self.cs, self.cr, self.ps, self.pr, self.zs, self.zr = bufs[3:]

    @staticmethod
    def scratch(n_dp, n_t, rb, cb):
        n_p = n_dp // 2
        return [
            pltpu.VMEM((n_t, n_p, rb, cb), BF), pltpu.VMEM((n_t, n_p - 1, rb, cb), BF),
            pltpu.VMEM((n_t - 1, rb, cb), BF),
            dma(n_t), dma(n_t), dma(n_t * (n_p - 1)), dma(n_t * (n_p - 1)), dma(n_t), dma(n_t - 1),
        ]

    def c_copy(self, c):
        p = self.p
        return remote(
            self.src.at[c, 1 - p.core], self.cb.at[c], self.cs.at[c], self.cr.at[c], p.sibling
        )

    def p_copy(self, c, s):
        p = self.p
        q, at = p.plane_up(s), c * (p.n_p - 1) + s - 1
        return remote(
            self.cb.at[c, q], self.pb.at[c, s - 1], self.ps.at[at], self.pr.at[at],
            (q * 2 + p.core, p.t),
        )

    def z_copy(self, c):
        p = self.p
        rel = jnp.maximum(lax.rem(p.t - c + p.n_t, p.n_t) - 1, 0)
        return remote(
            self.cb.at[c, p.plane], self.zb.at[rel], self.zs.at[c], self.zr.at[rel], (p.dp, c)
        )

    def start_c(self, c):
        self.c_copy(c).start()

    def start_p(self, c):
        p = self.p
        self.c_copy(c).wait_recv()
        for s in range(1, p.n_p):
            q = p.plane_up(s)
            self.cb[c, q] = (
                self.src[c, p.core, q].astype(F32) + self.cb[c, q].astype(F32)
            ).astype(BF)
            self.p_copy(c, s).start()

    def start_z(self, c):
        p = self.p
        total = self.src[c, p.core, p.plane].astype(F32) + self.cb[c, p.plane].astype(F32)
        for s in range(1, p.n_p):
            self.p_copy(c, s).wait_recv()
            total = total + self.pb[c, s - 1].astype(F32)

        @pl.when(p.t == c)
        def _():
            self.out[...] = total

        @pl.when(p.t != c)
        def _():
            self.cb[c, p.plane] = total.astype(BF)
            self.z_copy(c).start()

        self.c_copy(c).wait_send()

    def finish(self):
        p = self.p
        total = self.out[...]
        for s in range(1, p.n_t):
            view = self.zb.at[s - 1]
            remote(view, view, self.zs.at[0], self.zr.at[s - 1], p.sibling).wait_recv()
            total = total + self.zb[s - 1].astype(F32)
        self.out[...] = total

        @pl.loop(0, p.n_t)
        def _(c):
            for s in range(1, p.n_p):
                self.p_copy(c, s).wait_send()

            @pl.when(p.t != c)
            def _():
                self.z_copy(c).wait_send()


class Little:
    def __init__(self, place, src, out, bufs):
        self.p, self.src, self.out = place, src, out
        self.cb, self.pb, self.zo, self.zb = bufs[:4]
        self.cs, self.cr, self.ps, self.pr, self.zs, self.zr = bufs[4:]
        self.sent = []

    @staticmethod
    def scratch(n_dp, n_t, block, dtype):
        n_p = n_dp // 2
        return [
            pltpu.VMEM((n_p, n_t) + block, dtype), pltpu.VMEM((n_p - 1, n_t) + block, dtype),
            pltpu.VMEM((n_t,) + block, dtype), pltpu.VMEM((n_t - 1,) + block, dtype),
            dma(1), dma(1), dma(n_p - 1), dma(n_p - 1), dma(n_t - 1), dma(n_t - 1),
        ]

    go = Gather.go

    def start_c(self):
        p = self.p
        view = self.src.at[pl.ds((1 - p.core) * p.n_p, p.n_p)]
        self.go(view, self.cb, self.cs.at[0], self.cr.at[0], p.sibling)

    def start_p(self):
        p = self.p
        remote(self.cb, self.cb, self.cs.at[0], self.cr.at[0], p.sibling).wait_recv()
        for s in list(range(1, p.n_p)) + [0]:
            q = p.plane_up(s)

            @pl.loop(0, p.n_t)
            def _(t):
                own = self.src[p.core * p.n_p + q, t].astype(F32)
                self.cb[q, t] = (own + self.cb[q, t].astype(F32)).astype(self.cb.dtype)

            if s:
                self.go(
                    self.cb.at[q], self.pb.at[s - 1], self.ps.at[s - 1], self.pr.at[s - 1],
                    (q * 2 + p.core, p.t),
                )

    def start_z(self):
        p = self.p
        for s in range(1, p.n_p):
            view = self.pb.at[s - 1]
            remote(view, view, self.ps.at[s - 1], self.pr.at[s - 1], p.sibling).wait_recv()
        for s in list(range(1, p.n_t)) + [0]:
            t = p.up(s)
            total = self.cb[p.plane, t].astype(F32)
            for k in range(p.n_p - 1):
                total = total + self.pb[k, t].astype(F32)
            if s:
                self.zo[s] = total.astype(self.zo.dtype)
                self.go(
                    self.zo.at[s], self.zb.at[s - 1], self.zs.at[s - 1], self.zr.at[s - 1],
                    (p.dp, t),
                )
            else:
                self.out[...] = total

    def finish(self):
        p = self.p
        total = self.out[...]
        for s in range(1, p.n_t):
            view = self.zb.at[s - 1]
            remote(view, view, self.zs.at[s - 1], self.zr.at[s - 1], p.sibling).wait_recv()
            total = total + self.zb[s - 1].astype(F32)
        self.out[...] = total
        for copy in self.sent:
            copy.wait_send()


class Return(Undeal):
    def __init__(self, place, deal, src, out, bufs, spare, sem):
        super().__init__(place, deal, src, out, bufs)
        self.spare, self.sem = spare, sem

    def arrive(self):
        p = self.p
        for s in range(1, p.n_dp):
            view = self.buf.at[:, p.dp_down(s)]
            remote(view, view, self.ss.at[s - 1], self.rs.at[s - 1], p.sibling).wait_recv()
        self.moves = []
        for m in range(self.src.shape[0]):
            for k in range(p.n_dp):
                self.spare[k, m] = self.buf[m, self.deal[m, k]]
            move = pltpu.make_async_copy(self.spare.at[:, m], self.out.at[m], self.sem.at[m])
            move.start()
            self.moves.append(move)

    def finish(self):
        for copy in self.sent:
            copy.wait_send()
        for move in self.moves:
            move.wait()


class Rows(Gather):
    def slot(self, dp, t):
        rb = self.block[0]
        at = pl.multiple_of((dp * self.p.n_t + t) * rb, 8)
        return self.out.at[pl.ds(at, rb), :]

    def band(self, dp):
        rb = self.block[0] * self.p.n_t
        return self.out.at[pl.ds(pl.multiple_of(dp * rb, 8), rb), :]


class Relay:
    def __init__(self, place, rank, step, terms, keep, out, bufs):
        self.p, self.rank, self.terms, self.keep, self.out = place, rank, terms, keep, out
        self.buf, self.ss, self.rs = bufs
        self.to = (place.dp, jnp.clip(place.t + step, 0, place.n_t - 1))
        self.micro = terms.shape[0]
        self.count = terms.shape[0] * terms.shape[1]

    def copy(self, j):
        m, c = lax.rem(j, self.micro), lax.div(j, self.micro)
        view = self.out.at[m, c]
        return m, c, remote(self.buf.at[j], view, self.ss.at[j], self.rs.at[j], self.to)

    def step(self, k):
        j = k - LAG * self.rank

        @pl.when((j >= 0) & (j < self.count))
        def _():
            m, c, copy = self.copy(j)

            @pl.when(self.rank > 0)
            def _():
                copy.wait_recv()

            @pl.when(self.rank < self.p.n_t - 1)
            def _():
                self.buf[j] = (
                    self.terms[m, c].astype(F32)
                    + self.keep[m, c, 0:1] * self.out[m, c].astype(F32)
                ).astype(BF)
                copy.start()

    def finish(self):
        @pl.when(self.rank < self.p.n_t - 1)
        def _():
            @pl.loop(0, self.count)
            def _(j):
                self.copy(j)[2].wait_send()


def lanes_back(x, count):
    return pltpu.roll(x, lax.rem(LANES - count, LANES), x.ndim - 1)


def place_lanes(tiles, x, at, used):
    lane = iota(x.shape, x.ndim - 1)
    a, b = at // LANES, at % LANES
    x = jnp.where(lane < used, x, 0.0)
    if b:
        x = pltpu.roll(x, b, x.ndim - 1)
    if b + used > LANES:
        tiles[a] = tiles[a] + jnp.where(lane >= b, x, 0.0)
        tiles[a + 1] = tiles[a + 1] + jnp.where(lane < b, x, 0.0)
    else:
        tiles[a] = tiles[a] + x


def pick_lanes(x, at, used):
    a, b = at // LANES, at % LANES
    first = x[..., a * LANES : (a + 1) * LANES]
    if not b:
        return first
    first = pltpu.roll(first, LANES - b, first.ndim - 1)
    if b + used <= LANES:
        return first
    rest = pltpu.roll(x[..., (a + 1) * LANES : (a + 2) * LANES], LANES - b, first.ndim - 1)
    return jnp.where(iota(first.shape, first.ndim - 1) < LANES - b, first, rest)


def mega_scratch(n_dp, n_t, micro, rows, width, inner, rb, cb, wbc_rows, state, pack_shape):
    n_p, piece = n_dp // 2, rows // n_dp
    pieces = (micro, n_dp, piece, width)
    bands = (micro, n_t, rows, cb)
    v = pltpu.VMEM
    plain = [
        ("u", v(pieces, BF)), ("g", v(pieces, BF)), ("halo", v((micro, HALO, width), BF)),
        ("wx", v((width, inner), BF)), ("wz", v((width, inner), BF)), ("wo", v((width, inner), BF)),
        ("wbc", v((width, 2 * state), BF)), ("packs", v((n_dp, n_t) + pack_shape, F32)),
        ("kx", v((n_t, 8, cb), F32)), ("gain", v((8, width), F32)), ("kbc", v((8, 2 * state), F32)),
        ("hd", v((8, LANES), F32)), ("wdt", v((LANES, width), BF)),
        ("nrm", v((micro, rows + HALO, width), BF)), ("nt", v((width, micro * rows), BF)),
        ("nth", v((width, LANES), BF)), ("gt", v((width, micro * rows), BF)),
        ("far", v((micro, rows, LANES), F32)),
        ("xr", v((micro, n_t, rows + HALO, cb), BF)), ("bcr", v((micro, rows + HALO, 2 * state), F32)),
        ("xc", v(bands, BF)), ("xh", v(bands, BF)), ("dy", v(bands, BF)),
        ("yn", v(bands, F32)), ("z", v(bands, F32)),
        ("bc", v((micro, rows, 2 * state), BF)), ("bt", v((micro, state, rows), BF)),
        ("ct", v((micro, state, rows), BF)),
        ("cum", v((micro, rows, LANES), F32)), ("cumt", v((micro, LANES, rows), F32)),
        ("v", v((micro, rows, LANES), F32)), ("delta", v((micro, rows, LANES), F32)),
        ("lead", v((micro, rows, LANES), F32)), ("weight", v((micro, rows, LANES), F32)),
        ("keep8", v((micro, 8, LANES), F32)), ("keep", v((micro, n_t, 8, cb), F32)),
        ("sc", v((micro, rows, rows), F32)), ("sct", v((micro, rows, rows), F32)),
        ("dsc", v((micro, rows, rows), F32)),
        ("s", v((micro, n_t, state, cb), F32)), ("ds", v((micro, n_t, state, cb), BF)),
        ("hin", v((micro, n_t, state, cb), BF)), ("dso", v((micro, n_t, state, cb), BF)),
        ("en", v((micro, rows, LANES), F32)), ("ip", v((micro, rows, LANES), F32)),
        ("rd", v((micro, rows, LANES), F32)), ("col", v((micro, rows, LANES), F32)),
        ("last", v((micro, 8, LANES), F32)),
        ("db", v((micro, rows, state), F32)), ("dc", v((micro, rows, state), F32)),
        ("dzs", v((micro * rows, cb), BF)), ("normal", v((micro * rows, cb), BF)), ("dxh", v((micro * HALO, cb), BF)),
        ("oacc", v((micro, rows, width), F32)), ("dn", v((micro, rows + HALO, width), F32)),
        ("spill", v((micro, HALO, width), F32)),
        ("dk", v((n_t, 8, cb), F32)), ("dkbc", v((8, 2 * state), F32)), ("ddt", v((8, LANES), F32)),
        ("dpre", v((8, width), F32)),
        ("dwo", v((n_t, 2, n_p, rb, cb), BF)), ("dwz", v((n_t, 2, n_p, rb, cb), BF)),
        ("dwbc", v((n_dp, n_t, wbc_rows, 2 * state), BF)), ("ddtb", v((micro * rows, LANES), BF)),
        ("orows", v(pieces, BF)),
    ]
    count = micro * n_t
    groups = [
        ("ag_pack", Gather.scratch(n_dp, n_t)), ("ag_bc", Gather.scratch(n_dp, n_t)),
        ("ag_x", Gather.scratch(n_dp, n_t)), ("ag_z", Gather.scratch(n_dp, n_t)),
        ("ag_o", Gather.scratch(n_dp, n_t)),
        ("deal_u", Deal.scratch(n_dp, pieces)), ("deal_g", Deal.scratch(n_dp, pieces)[1:]),
        ("halo_s", [dma(1), dma(1)]), ("spill_s", [dma(1), dma(1)]),
        ("chain_f", [v((count, state, cb), BF), dma(count), dma(count)]),
        ("chain_b", [dma(count), dma(count)]),
        ("rs_o", Sums.scratch(n_dp, n_t, rb, cb)), ("rs_z", Sums.scratch(n_dp, n_t, rb, cb)),
        ("rs_x", Sums.scratch(n_dp, n_t, rb, cb)),
        ("rs_bc", Little.scratch(n_dp, n_t, (wbc_rows, 2 * state), BF)),
        ("rs_pack", Little.scratch(n_dp, n_t, pack_shape, F32)),
        ("back_o", Undeal.scratch(n_dp, pieces)), ("back_t", Undeal.scratch(n_dp, pieces)),
        ("back_s", [dma(micro), dma(micro)]), ("in_s", [dma(2)]),
    ]
    return plain, groups


def mega_kernel(
    n_dp, n_t, sizes, names, group_sizes, lens, order, deal, tokens, cot, w_x, w_z, w_o, w_bc, pack,
    output, d_tokens, o_x, o_z, o_o, o_bc, o_pack, *scratch,
):
    size, state, taps, seqs, per_t, size_d = sizes
    p = Place(n_dp, n_t)
    refs = dict(zip(names, scratch[: len(names)]))
    at, groups = len(names), {}
    for name, count in group_sizes:
        groups[name] = scratch[at : at + count]
        at += count
    r = lambda name: refs[name]
    u, g, wx, wz, wo = r("u"), r("g"), r("wx"), r("wz"), r("wo")
    nrm, xr, xc_s, xh_s = r("nrm"), r("xr"), r("xc"), r("xh")
    micro, _, piece, width = u.shape
    rows = n_dp * piece
    cb = w_x.shape[1]
    rb = w_x.shape[0]
    inner = cb * n_t
    steps = micro * n_t
    pos0 = p.t * rows
    heads_at = 8
    pair = LANES // size
    lane = iota((rows, LANES), 1)
    ones = reducer(0, size, cb)

    ag_pack = Gather(p, pack, r("packs"), groups["ag_pack"])
    ag_bc = Rows(p, w_bc, r("wbc"), groups["ag_bc"])
    ag_x = Gather(p, w_x, wx, groups["ag_x"])
    ag_z = Gather(p, w_z, wz, groups["ag_z"])
    ag_o = Gather(p, w_o, wo, groups["ag_o"])
    staged, in_sem = r("orows"), groups["in_s"][0]
    bring_u = pltpu.make_async_copy(tokens, staged, in_sem.at[0])
    bring_g = pltpu.make_async_copy(cot, staged, in_sem.at[1])
    deal_u = Deal(p, order, staged, u, groups["deal_u"])
    deal_g = Deal(p, order, staged, g, groups["deal_u"][:1] + groups["deal_g"])
    halo = Halo(p, 1, r("halo"), groups["halo_s"])
    chain_f = Relay(p, p.t, 1, r("s"), r("keep"), r("hin"), groups["chain_f"])
    chain_b = Relay(p, n_t - 1 - p.t, -1, r("ds"), r("keep"), r("dso"), groups["chain_f"][:1] + groups["chain_b"])
    rs_o = Sums(p, r("dwo"), o_o, groups["rs_o"])
    rs_z = Sums(p, r("dwz"), o_z, groups["rs_z"])
    rs_x = Sums(p, r("dwo"), o_x, groups["rs_x"])
    rs_bc = Little(p, r("dwbc"), o_bc, groups["rs_bc"])
    rs_pack = Little(p, r("packs"), o_pack, groups["rs_pack"])
    spare, (out_sem, tok_sem) = groups["deal_u"][0], groups["back_s"]
    back_o = Return(p, deal, r("orows"), output, groups["back_o"], spare, out_sem)
    back_t = Return(p, deal, r("orows"), d_tokens, groups["back_t"], spare, tok_sem)
    spill = Halo(p, -1, r("spill"), groups["spill_s"])

    bring_u.start()
    p.barrier()
    ag_pack.start_z()
    ag_bc.start_z()
    ag_x.start_z()
    bring_u.wait()
    deal_u.start()
    bring_g.start()
    ag_pack.start_p()
    ag_bc.start_p()
    ag_x.start_p()
    ag_z.start_z()
    ag_o.start_z()

    @pl.when(p.t == 0)
    def _():
        r("hin")[...] = jnp.zeros(r("hin").shape, BF)

    @pl.when(p.t == n_t - 1)
    def _():
        r("dso")[...] = jnp.zeros(r("dso").shape, BF)

    for name in ("en", "ip", "rd", "col", "last", "db", "dc", "dk", "dkbc", "ddt", "dsc", "dn", "dpre"):
        refs[name][...] = jnp.zeros(refs[name].shape, F32)
    r("nth")[...] = jnp.zeros((width, LANES), BF)
    bounds = [bounds_of(lens, m, seqs) for m in range(micro)]
    for m in range(micro):
        r("far")[m] = reach(bounds[m], pos0, rows, taps)

    deal_u.finish()
    halo.start(u.at[:, n_dp - 1, piece - HALO : piece, :])
    ag_pack.start_c()
    ag_bc.start_c()
    bring_g.wait()
    deal_g.start()
    ag_x.start_c()
    ag_pack.finish()

    packs = r("packs")
    pairs = per_t // pair
    base = pairs * 8
    gain_t = [jnp.zeros((8, LANES), F32) for _ in range(width // LANES)]
    kbc_t = [jnp.zeros((8, LANES), F32) for _ in range(2 * state // LANES)]
    hd_t = [[jnp.zeros((1, LANES), F32)] for _ in range(3)]
    wdt_t = [jnp.zeros((n_t * 8, LANES), F32) for _ in range(width // LANES)]
    per_gain, per_bc = width // (n_dp * n_t), 2 * state // (n_dp * n_t)
    for t in range(n_t):
        for q in range(pairs):
            tile = packs[0, t, q * 8 : (q + 1) * 8]
            for dp in range(1, n_dp):
                tile = tile + packs[dp, t, q * 8 : (q + 1) * 8]
            r("kx")[t, :, q * LANES : (q + 1) * LANES] = tile
        row = packs[0, t, base + 6 : base + 7]
        for q in range(3):
            place_lanes(hd_t[q], pltpu.roll(row, LANES - 8 * q, 1) if q else row, t * 8, 8)
        for dp in range(n_dp):
            tile = packs[dp, t, base : base + 8]
            place_lanes(gain_t, tile, (dp * n_t + t) * per_gain, per_gain)
            place_lanes(kbc_t, tile, (dp * n_t + t) * per_bc, per_bc)
    for dp in range(n_dp):
        tile = packs[dp, :, base + 8 : base + 16].reshape(n_t * 8, LANES)
        place_lanes(wdt_t, tile, dp * rb, rb)
    r("gain")[...] = jnp.concatenate(gain_t, axis=1)
    r("kbc")[...] = jnp.concatenate(kbc_t, axis=1)
    r("wdt")[...] = jnp.zeros((LANES, width), BF)
    r("wdt")[: n_t * 8] = jnp.concatenate(wdt_t, axis=1).astype(BF)
    for q in range(3):
        r("hd")[q : q + 1] = hd_t[q][0]
    skip8 = jnp.broadcast_to(r("hd")[2:3], (8, LANES))
    for t in range(n_t):
        r("kx")[t, 6:7] = expand(lanes_back(skip8, 8 * t), 0, per_t, size)[0:1]
    dtb, alog = r("hd")[0:1], r("hd")[1:2]
    rate_of = -jnp.exp(alog)
    gain = r("gain")[0:1]

    def norm(v):
        v = v.astype(F32)
        q = lax.rsqrt(jnp.mean(v * v, axis=1, keepdims=True) + EPS)
        return (v * q * gain).astype(BF)

    for m in range(micro):
        nrm[m, HALO:] = norm(u[m].reshape(rows, width))
        r("nt")[:, m * rows : (m + 1) * rows] = nrm[m, HALO:].astype(F32).T.astype(BF)
    halo.finish()
    pad = jnp.zeros((LANES - micro * HALO, width), F32)
    tails = []
    for m in range(micro):
        nrm[m, :HALO] = norm(r("halo")[m])
        tails.append(nrm[m, :HALO].astype(F32))
    r("nth")[...] = jnp.concatenate(tails + [pad], axis=0).T.astype(BF)

    ag_bc.finish()
    for m in range(micro):
        vv = dot_nt(nrm[m, HALO:], r("wdt")[...]) + dtb
        r("v")[m] = vv
        delta = softplus(vv)
        r("delta")[m] = delta
        cum = prefix_rows(delta * rate_of)
        r("cum")[m] = cum
        r("cumt")[m] = cum.T
        end = cum[rows - 1 : rows]
        tail_seg = seg_of(pos0 + rows - 1, bounds[m])
        last_seg = seg_of(pos0 - 1, bounds[m])
        here = seg_of(pos0 + iota((rows, LANES), 0), bounds[m])
        r("weight")[m] = jnp.exp(end - cum) * (here == tail_seg).astype(F32)
        r("lead")[m] = jnp.exp(cum) * (here == last_seg).astype(F32)
        r("keep8")[m] = jnp.exp(jnp.broadcast_to(end, (8, LANES))) * jnp.where(
            tail_seg == last_seg, 1.0, 0.0
        )
        bcr = dot_nn(nrm[m], r("wbc")[...])
        r("bcr")[m] = bcr
        far = r("far")[m]
        pre = conv(bcr, r("kbc")[1 : 1 + taps], r("kbc")[1 + taps : 2 + taps], far, taps)
        bc = (pre * sigmoid(pre)).astype(BF)
        r("bc")[m] = bc
        r("bt")[m] = bc[:, :state].astype(F32).T.astype(BF)
        r("ct")[m] = bc[:, state:].astype(F32).T.astype(BF)
        t_at, s_at = iota((rows, rows), 0), iota((rows, rows), 1)
        same = seg_of(pos0 + t_at, bounds[m]) == seg_of(pos0 + s_at, bounds[m])
        scores = dot_nt(bc[:, state:], bc[:, :state])
        r("sc")[m] = jnp.where((t_at >= s_at) & same, scores, 0.0)
        r("sct")[m] = jnp.where((t_at <= s_at) & same, dot_nt(bc[:, :state], bc[:, state:]), 0.0)
    ag_z.start_p()
    ag_x.finish()

    def where_at(k):
        return lax.div(k, micro), lax.rem(k, micro)

    def cols(w, c):
        return w[:, pl.ds(pl.multiple_of(c * cb, LANES), cb)]

    def heads_of(name, m, c):
        return lanes_back(refs[name][m], heads_at * c)

    @pl.loop(0, steps)
    def _(k):
        c, m = where_at(k)
        x = dot_nn(nrm[m], cols(wx, c))
        xr[m, c] = x.astype(BF)
        far = r("far")[m]
        kx = r("kx")[c]
        pre = conv(x, kx, kx[taps : taps + 1], far, taps)
        xc = pre * sigmoid(pre)
        xc_s[m, c] = xc.astype(BF)
        xh = (xc * expand(heads_of("delta", m, c), 0, per_t, size)).astype(BF)
        xh_s[m, c] = xh
        xt = (xh.astype(F32) * expand(heads_of("weight", m, c), 0, per_t, size)).astype(BF)
        r("s")[m, c] = dot_nn(r("bt")[m], xt)
        r("keep")[m, c] = expand(heads_of("keep8", m, c), 0, per_t, size)
        chain_f.step(k)

    ag_o.start_p()
    ag_z.start_c()
    ag_z.finish()

    @pl.loop(0, steps)
    def _(k):
        c, m = where_at(k)
        col, row = heads_of("cum", m, c), r("cumt")[m, pl.ds(pl.multiple_of(c * 8, 8), 8)]
        scores = r("sc")[m]
        for j in range(pairs):
            xp = xh_s[m, c, :, j * LANES : (j + 1) * LANES]
            block = None
            for i in range(pair):
                h = j * pair + i
                mix = (scores * decay_block(col[:, h : h + 1], row[h : h + 1])).astype(BF)
                part = dot_nn(mix, xp)
                block = part if block is None else jnp.where(lane >= i * size, part, block)
            r("yn")[m, c, :, j * LANES : (j + 1) * LANES] = block
        r("z")[m, c] = dot_nn(nrm[m, HALO:], cols(wz, c))
        chain_f.step(k + steps)

    ag_o.start_c()

    @pl.loop(2 * steps, max(2 * steps, steps + LAG * (n_t - 1)) + 1)
    def _(k):
        chain_f.step(k)

    chain_f.finish()
    deal_g.finish()
    for m in range(micro):
        r("gt")[:, m * rows : (m + 1) * rows] = (
            g[m].reshape(rows, width).astype(F32).T.astype(BF)
        )
    ag_o.finish()

    @pl.loop(0, steps)
    def _(k):
        c, m = where_at(k)
        kx = r("kx")[c]
        cm = r("bc")[m, :, state:]
        yn = r("yn")[m, c] + dot_nn(cm, r("hin")[m, c]) * expand(
            heads_of("lead", m, c), 0, per_t, size
        )
        r("yn")[m, c] = yn
        z = r("z")[m, c]
        gated = (yn + kx[6:7] * xc_s[m, c].astype(F32)) * (z * sigmoid(z))
        d_normal = dot_nn(g[m].reshape(rows, width), cols(wo, c))
        prod = d_normal * kx[5:6] * gated
        en, ip = r("en")[m], r("ip")[m]
        for j in range(cb // LANES):
            piece_g = gated[:, j * LANES : (j + 1) * LANES]
            en = en + piece_g * piece_g
            ip = ip + prod[:, j * LANES : (j + 1) * LANES]
        r("en")[m] = en
        r("ip")[m] = ip

    for m in range(micro):
        rinv = lax.rsqrt(jnp.sum(r("en")[m], axis=1, keepdims=True) / inner + EPS)
        slope = rinv * rinv * rinv * (jnp.sum(r("ip")[m], axis=1, keepdims=True) / inner)
        r("en")[m] = jnp.broadcast_to(rinv, (rows, LANES))
        r("ip")[m] = jnp.broadcast_to(slope, (rows, LANES))
        r("oacc")[m] = u[m].reshape(rows, width).astype(F32)

    def into_bands(out, c, total):
        for dp in range(n_dp):
            out[c, dp % 2, dp // 2] = total[dp * rb : (dp + 1) * rb].astype(BF)

    @pl.loop(0, steps)
    def _(k):
        c, m = where_at(k)
        kx = r("kx")[c]
        yn = r("yn")[m, c]
        z = r("z")[m, c]
        sg = sigmoid(z)
        gate = z * sg
        xc = xc_s[m, c].astype(F32)
        y = yn + kx[6:7] * xc
        gated = y * gate
        rinv, slope = wide(r("en")[m], cb), wide(r("ip")[m], cb)
        scaled = gated * rinv
        normal = (scaled * kx[5:6]).astype(BF)
        r("normal")[pl.ds(pl.multiple_of(m * rows, rows), rows)] = normal
        r("oacc")[m] += dot_nt(normal, cols(wo, c))
        d_normal = dot_nn(g[m].reshape(rows, width), cols(wo, c))
        d_gated = rinv * (d_normal * kx[5:6]) - gated * slope
        r("dk")[c, 5:6] += jnp.sum(d_normal * scaled, axis=0, keepdims=True)
        dz = (d_gated * y * (sg * (1.0 + z * (1.0 - sg)))).astype(BF)
        r("dzs")[pl.ds(pl.multiple_of(m * rows, rows), rows)] = dz
        dyb = (d_gated * gate).astype(BF)
        r("dy")[m, c] = dyb
        dyf = dyb.astype(F32)
        r("rd")[m] += pltpu.roll(head_sums(dyf * yn, ones), heads_at * c, 1)
        r("dk")[c, 6:7] += jnp.sum(dyf * xc, axis=0, keepdims=True)
        r("ds")[m, c] = dot_nn(
            r("ct")[m], (dyf * expand(heads_of("lead", m, c), 0, per_t, size)).astype(BF)
        ).astype(BF)
        r("dn")[m, HALO:] += dot_nt(dz, cols(wz, c))
        chain_b.step(k)

        @pl.when(m == micro - 1)
        def _():
            into_bands(r("dwo"), c, dot_nn(r("gt")[...], r("normal")[...]))
            rs_o.start_c(c)
            into_bands(r("dwz"), c, dot_nn(r("nt")[...], r("dzs")[...]))
            rs_z.start_c(c)

    for m in range(micro):
        r("orows")[m] = r("oacc")[m].astype(BF).reshape(n_dp, piece, width)
    back_o.start()

    @pl.loop(0, steps)
    def _(k):
        c, m = where_at(k)
        col, row = heads_of("cum", m, c), r("cumt")[m, pl.ds(pl.multiple_of(c * 8, 8), 8)]
        scores = r("sct")[m]
        d_scores = r("dsc")[m]
        for j in range(pairs):
            span = slice(j * LANES, (j + 1) * LANES)
            xp, dyp = xh_s[m, c, :, span], r("dy")[m, c, :, span]
            block = None
            for i in range(pair):
                h = j * pair + i
                fall = decay_block(row[h : h + 1], col[:, h : h + 1])
                part = dot_nn((scores * fall).astype(BF), dyp)
                block = part if block is None else jnp.where(lane >= i * size, part, block)
                mine = (lane >= i * size) & (lane < (i + 1) * size)
                d_scores = d_scores + dot_nt(jnp.where(mine, xp, 0), dyp) * fall
            r("yn")[m, c, :, span] = block
        r("dsc")[m] = d_scores
        chain_b.step(k + steps)

        @pl.when(m == 0)
        def _():
            rs_o.start_p(c)

        @pl.when(m == micro - 1)
        def _():
            rs_z.start_p(c)

    @pl.loop(2 * steps, max(2 * steps, steps + LAG * (n_t - 1)) + 1)
    def _(k):
        chain_b.step(k)

    @pl.loop(0, steps)
    def _(k):
        c, m = where_at(k)
        kx = r("kx")[c]
        bm = r("bc")[m, :, :state]
        wide_w = expand(heads_of("weight", m, c), 0, per_t, size)
        intra = r("yn")[m, c]
        xhf = xh_s[m, c].astype(F32)
        dso = r("dso")[m, c]
        passed = dot_nn(bm, dso)
        xt = (xhf * wide_w).astype(BF)
        r("col")[m] += pltpu.roll(
            head_sums(xhf * intra + xt.astype(F32) * passed, ones), heads_at * c, 1
        )
        r("db")[m] += dot_nt(xt, dso)
        dyf = r("dy")[m, c].astype(F32)
        hin = r("hin")[m, c]
        r("dc")[m] += dot_nt(
            (dyf * expand(heads_of("lead", m, c), 0, per_t, size)).astype(BF), hin
        )
        s_out = r("s")[m, c] + r("keep")[m, c, 0:1] * hin.astype(F32)
        both = jnp.sum(dso.astype(F32) * s_out, axis=0, keepdims=True)
        r("last")[m] += pltpu.roll(
            head_sums(jnp.broadcast_to(both, (8, cb)), ones), heads_at * c, 1
        )
        d_xc = (intra + passed * wide_w) * expand(heads_of("delta", m, c), 0, per_t, size)
        d_xc = d_xc + kx[6:7] * dyf
        ext = xr[m, c].astype(F32)
        far = r("far")[m]
        pre = conv(ext, kx, kx[taps : taps + 1], far, taps)
        sg = sigmoid(pre)
        dpre = d_xc * (sg * (1.0 + pre * (1.0 - sg)))
        d_ext, d_kernel = conv_back(ext, dpre, kx, far, taps)
        for i in range(taps):
            r("dk")[c, i : i + 1] += d_kernel[i]
        r("dk")[c, taps : taps + 1] += jnp.sum(dpre, axis=0, keepdims=True)
        dxr = d_ext.astype(BF)
        r("dn")[m] += dot_nt(dxr, cols(wx, c))
        r("dzs")[pl.ds(pl.multiple_of(m * rows, rows), rows)] = dxr[HALO:]
        r("dxh")[pl.ds(pl.multiple_of(m * HALO, HALO), HALO)] = dxr[:HALO]

        @pl.when(m == 0)
        def _():
            rs_o.start_z(c)

        @pl.when(m == micro - 1)
        def _():
            total = dot_nn(r("nt")[...], r("dzs")[...])
            total = total + dot_nn(r("nth")[:, : micro * HALO], r("dxh")[...])
            into_bands(r("dwo"), c, total)
            rs_x.start_c(c)
            rs_z.start_z(c)

    rs_x.start_p(0)
    rs_x.start_p(1)
    dwbc = jnp.zeros((width, 2 * state), F32)
    for m in range(micro):
        t_at, s_at = iota((rows, rows), 1), iota((rows, rows), 0)
        same = seg_of(pos0 + t_at, bounds[m]) == seg_of(pos0 + s_at, bounds[m])
        d_scores = jnp.where((t_at >= s_at) & same, r("dsc")[m], 0.0)
        bm, cm = r("bc")[m, :, :state], r("bc")[m, :, state:]
        d_b = r("db")[m] + dot_nn(d_scores.astype(BF), cm)
        d_c = r("dc")[m] + dot_nn(d_scores.T.astype(BF), bm)
        d_bc = jnp.concatenate([d_b, d_c], axis=1)
        ext = r("bcr")[m]
        far = r("far")[m]
        kbc = r("kbc")[1 : 1 + taps]
        pre = conv(ext, kbc, r("kbc")[1 + taps : 2 + taps], far, taps)
        sg = sigmoid(pre)
        dpre = d_bc * (sg * (1.0 + pre * (1.0 - sg)))
        d_ext, d_kernel = conv_back(ext, dpre, kbc, far, taps)
        for i in range(taps):
            r("dkbc")[1 + i : 2 + i] += d_kernel[i]
        r("dkbc")[1 + taps : 2 + taps] += jnp.sum(dpre, axis=0, keepdims=True)
        dbcr = d_ext.astype(BF)
        r("dn")[m] += dot_nt(dbcr, r("wbc")[...])
        dwbc = dwbc + dot_nn(r("nt")[:, m * rows : (m + 1) * rows], dbcr[HALO:])
        dwbc = dwbc + dot_nn(r("nth")[:, m * HALO : (m + 1) * HALO], dbcr[:HALO])
        row = iota((rows, LANES), 0)
        d_cum = r("rd")[m] - r("col")[m]
        d_cum = d_cum + jnp.where(
            row == rows - 1, jnp.broadcast_to(r("last")[m, 0:1], (rows, LANES)), 0.0
        )
        d_rate = suffix_rows(d_cum)
        delta, sg_dt = r("delta")[m], sigmoid(r("v")[m])
        ratio = jnp.where(delta > 1e-30, sg_dt / jnp.maximum(delta, 1e-30), 1.0)
        d_dt = r("col")[m] * ratio + d_rate * rate_of * sg_dt
        r("ddt")[0:1] += jnp.sum(d_dt, axis=0, keepdims=True)
        r("ddt")[1:2] += jnp.sum(d_rate * delta * rate_of, axis=0, keepdims=True)
        d_dtb = d_dt.astype(BF)
        r("ddtb")[m * rows : (m + 1) * rows] = d_dtb
        r("dn")[m, HALO:] += dot_nn(d_dtb, r("wdt")[...])
    spill.start(r("dn").at[:, :HALO, :])
    wb = w_bc.shape[0]
    for dp in range(n_dp):
        for t in range(n_t):
            at_row = (dp * n_t + t) * wb
            r("dwbc")[dp % 2 * p.n_p + dp // 2, t] = dwbc[at_row : at_row + wb].astype(BF)
    rs_bc.start_c()
    rs_x.start_p(2)
    rs_x.start_z(0)
    rs_x.start_p(3)
    rs_x.start_z(1)

    d_wdt = dot_nn(r("ddtb")[...].astype(F32).T.astype(BF), jnp.concatenate(
        [nrm[m, HALO:] for m in range(micro)], axis=0
    ))
    spill.finish()
    back_o.arrive()
    back_o.finish()
    for m in range(micro):
        r("dn")[m, rows:] += r("spill")[m]
        dn = r("dn")[m, HALO:]
        uf = u[m].reshape(rows, width).astype(F32)
        q = lax.rsqrt(jnp.mean(uf * uf, axis=1, keepdims=True) + EPS)
        f = dn * gain
        d_u = q * f - uf * (q * q * q * (jnp.sum(f * uf, axis=1, keepdims=True) / width))
        r("dpre")[0:1] += jnp.sum(dn * uf * q, axis=0, keepdims=True)
        total = g[m].reshape(rows, width).astype(F32) + d_u
        r("orows")[m] = total.astype(BF).reshape(n_dp, piece, width)
    back_t.start()

    dpack = r("packs")
    skips = jnp.zeros((8, LANES), F32)
    for t in range(n_t):
        part = head_sums(r("dk")[t], ones)
        skips = skips + pltpu.roll(part, 8 * t, 1) if t else skips + part
    lane8 = iota((8, LANES), 1)
    row8 = iota((8, LANES), 0)
    dkbc, dpre_g = r("dkbc")[...], r("dpre")[...]
    for t in range(n_t):
        heads = [lanes_back(x, 8 * t) for x in (r("ddt")[0:1], r("ddt")[1:2], skips[6:7])]
        line = jnp.where(
            lane8[0:1] < 8, heads[0],
            jnp.where(lane8[0:1] < 16, pltpu.roll(heads[1], 8, 1), pltpu.roll(heads[2], 16, 1)),
        )
        for dp in range(n_dp):
            off = dp * n_t + t
            for q in range(pairs):
                dpack[dp % 2 * p.n_p + dp // 2, t, q * 8 : (q + 1) * 8] = r("dk")[
                    t, :, q * LANES : (q + 1) * LANES
                ]
            tile = pick_lanes(dkbc, off * per_bc, per_bc)
            first = pick_lanes(dpre_g, off * per_gain, per_gain)
            tile = jnp.where(row8 == 0, first, tile)
            dpack[dp % 2 * p.n_p + dp // 2, t, base : base + 8] = jnp.where(
                row8 == 6, jnp.broadcast_to(line, (8, LANES)), tile
            )
            dpack[dp % 2 * p.n_p + dp // 2, t, base + 8 : base + 16] = pick_lanes(
                d_wdt[t * 8 : (t + 1) * 8], dp * rb, rb
            )
    rs_pack.start_c()
    rs_bc.start_p()
    rs_pack.start_p()
    rs_x.start_z(2)
    rs_x.start_z(3)
    rs_bc.start_z()
    rs_pack.start_z()
    rs_o.finish()
    rs_z.finish()
    chain_b.finish()
    rs_x.finish()
    rs_bc.finish()
    rs_pack.finish()
    o_pack[:base] = lanes_back(o_pack[:base], size_d * p.dp)
    back_t.arrive()
    back_t.finish()


def fused(
    tokens, lens, deal, order, cotangent, pre_gain, w_z, w_x, w_bc, w_dt, conv_x, conv_bx, conv_bc,
    conv_bbc, dt_bias, a_log, d_skip, norm_gain, w_out,
):
    micro, rows, width = tokens.shape
    n_dp, n_t = lax.axis_size("dp"), lax.axis_size("tensor")
    mine = lax.axis_index("dp")
    taps, per_t, size_d = conv_x.shape
    rb, cb = w_x.shape
    size, inner = size_d * n_dp, cb * n_t
    state = conv_bc.shape[1] * n_dp * n_t // 2
    pairs = per_t // 2
    base = pairs * 8
    stacked = jnp.concatenate(
        [conv_x, conv_bx[None], norm_gain[None], jnp.zeros((8 - taps - 2, per_t, size_d), BF)], axis=0
    )
    stacked = stacked.reshape(8, pairs, 2, 1, size_d).transpose(1, 0, 2, 3, 4).astype(F32)
    here = (jnp.arange(n_dp) == mine)[:, None]
    stacked = jnp.where(here, stacked, 0.0).reshape(base, LANES)
    per_bc = conv_bc.shape[1]
    line = jnp.concatenate(
        [jnp.pad(x, (0, 8 - per_t)) for x in (dt_bias, a_log, d_skip)]
    )
    small = jnp.concatenate(
        [
            pad_lanes(pre_gain[None].astype(F32)), pad_lanes(conv_bc.astype(F32)),
            pad_lanes(conv_bbc[None].astype(F32)), pad_lanes(line[None]), jnp.zeros((1, LANES), F32),
        ],
        axis=0,
    )
    steps_w = jnp.pad(w_dt.T.astype(F32), [(0, 8 - per_t), (0, LANES - rb)])
    pack = jnp.concatenate([stacked, small, steps_w], axis=0)
    pieces = (micro, n_dp, rows // n_dp, width)
    sizes = (size, state, taps, lens.shape[1], per_t, size_d)
    plain, groups = mega_scratch(
        n_dp, n_t, micro, rows, width, inner, rb, cb, w_bc.shape[0], state, pack.shape
    )
    kernel = functools.partial(
        mega_kernel, n_dp, n_t, sizes, [n for n, _ in plain], [(n, len(s)) for n, s in groups]
    )
    output, d_tokens, sum_x, sum_z, sum_o, sum_bc, sums = pl.pallas_call(
        kernel,
        in_specs=[SCALARS] * 3 + [IN_PLACE] * 7,
        out_specs=[IN_PLACE] * 2 + [IN_VMEM] * 5,
        out_shape=[
            jax.ShapeDtypeStruct(pieces, BF), jax.ShapeDtypeStruct(pieces, BF),
            jax.ShapeDtypeStruct((rb, cb), F32), jax.ShapeDtypeStruct((rb, cb), F32),
            jax.ShapeDtypeStruct((rb, cb), F32), jax.ShapeDtypeStruct(w_bc.shape, F32),
            jax.ShapeDtypeStruct(pack.shape, F32),
        ],
        scratch_shapes=[s for _, s in plain] + [x for _, s in groups for x in s],
        compiler_params=pltpu.CompilerParams(
            collective_id=7, has_side_effects=True, vmem_limit_bytes=MEGA_LIMIT
        ),
    )(
        lens, order, deal, tokens.reshape(pieces), cotangent.reshape(pieces), w_x, w_z, w_out.T, w_bc,
        pack,
    )
    got = sums[:base].reshape(pairs, 8, 2, LANES // 2)[:, :, :, :size_d]
    got = got.transpose(1, 0, 2, 3).reshape(8, per_t, size_d)
    small = sums[base : base + 8]
    d_dt = sums[base + 8 : base + 8 + per_t, :rb].T
    return (
        output.reshape(tokens.shape), d_tokens.reshape(tokens.shape), small[0, : pre_gain.shape[0]],
        sum_z, sum_x, sum_bc, d_dt, got[:taps], got[taps], small[1 : 1 + taps, :per_bc],
        small[1 + taps, :per_bc], small[6, :per_t], small[6, 8 : 8 + per_t],
        small[6, 16 : 16 + per_t], got[taps + 1], sum_o.T,
    )


def by_micro(shape):
    return pl.BlockSpec((1,) + tuple(shape[1:]), lambda m: (m,) + (0,) * (len(shape) - 1))


def whole(shape):
    return pl.BlockSpec(tuple(shape), lambda m: (0,) * len(shape))


SCALARS = pl.BlockSpec(memory_space=pltpu.SMEM)


def call(kernel, dims, micro, scalars, per_micro, shared, outs, scratch):
    in_specs = (
        [SCALARS] * len(scalars)
        + [by_micro(x.shape) for x in per_micro]
        + [whole(x.shape) for x in shared]
    )
    out_specs = [by_micro(s) if split else whole(s) for s, _, split in outs]
    return pl.pallas_call(
        functools.partial(kernel, dims),
        grid=(micro,),
        in_specs=in_specs,
        out_specs=out_specs,
        out_shape=[jax.ShapeDtypeStruct(s, d) for s, d, _ in outs],
        scratch_shapes=[pltpu.VMEM(s, d) for s, d in scratch],
        compiler_params=pltpu.CompilerParams(vmem_limit_bytes=VMEM_LIMIT),
    )(*scalars, *per_micro, *shared)


def pad_lanes(x, width=LANES):
    return jnp.pad(x, [(0, 0)] * (x.ndim - 1) + [(0, width - x.shape[-1])])


def pad_rows(x, rows=8):
    return jnp.pad(x, [(0, rows - x.shape[0])] + [(0, 0)] * (x.ndim - 1))


def local(
    tokens, lengths, dealing, cotangent, pre_gain, w_z, w_x, w_bc, w_dt, conv_x, conv_bx, conv_bc,
    conv_bbc, dt_bias, a_log, d_skip, norm_gain, w_out,
):
    micro, rows, width = tokens.shape
    n_dp, n_t = lax.axis_size("dp"), lax.axis_size("tensor")
    place = lax.axis_index("tensor")
    piece = rows // n_dp
    deal = dealing[:, 0, :]
    lens = lengths[:, 0, :]
    pos0 = (place * rows).reshape(1).astype(jnp.int32)

    slots = jnp.arange(n_dp, dtype=jnp.int32)
    deal = deal.astype(jnp.int32)
    order = jnp.sum(
        jnp.where(deal[:, None, :] == slots[None, :, None], slots[None, None, :], 0), axis=2
    )
    pieces = (micro, n_dp, piece, width)
    rb, cb = w_x.shape
    aligned = rb % 16 == 0 and cb % LANES == 0
    inner = cb * n_t
    taps, per_t, size_d = conv_x.shape
    heads, size = per_t * n_t, size_d * n_dp
    state = conv_bc.shape[1] * n_dp * n_t // 2
    seqs = lens.shape[1]
    dims = (heads, size, state, taps, seqs)

    if aligned and w_bc.shape[0] % 8 == 0 and per_t % 2 == 0 and per_t <= 8 and rb <= LANES:
        return fused(
            tokens, lens, deal, order, cotangent, pre_gain, w_z, w_x, w_bc, w_dt, conv_x, conv_bx,
            conv_bc, conv_bbc, dt_bias, a_log, d_skip, norm_gain, w_out,
        )
    lengths_of = [
        (taps + 2) * per_t * size_d, pre_gain.shape[0], (taps + 1) * conv_bc.shape[1],
        w_dt.shape[0] * per_t, 3 * per_t,
    ]
    used = sum(lengths_of)
    total = -(-used // 1024) * 1024
    stacked = jnp.concatenate([conv_x, conv_bx[None], norm_gain[None]], axis=0)
    bc_small = jnp.concatenate([conv_bc, conv_bbc[None]], axis=0)
    pack = jnp.concatenate(
        [
            stacked.reshape(-1).astype(F32), pre_gain.astype(F32), bc_small.reshape(-1).astype(F32),
            w_dt.reshape(-1).astype(F32), dt_bias, a_log, d_skip, jnp.zeros((total - used,), F32),
        ]
    ).reshape(total // LANES, LANES)
    starts = [0]
    for length in lengths_of:
        starts.append(starts[-1] + length)

    def gathered(shape, dtype):
        full_shape = (shape[0] * n_dp, shape[1] * n_t)
        return (full_shape if aligned else (n_dp, n_t) + shape, dtype, IN_PLACE)

    def joined(w):
        return w if aligned else w.transpose(0, 2, 1, 3).reshape(rb * n_dp, inner)

    u, halo, wx, wbc, packs = talk(
        enter_kernel, n_dp, n_t, 1, (order, tokens.reshape(pieces), w_x, w_bc, pack),
        [SCALARS, IN_VMEM, IN_PLACE, IN_PLACE, IN_PLACE],
        [
            (pieces, BF, IN_VMEM), ((micro, HALO, width), BF, IN_VMEM), gathered((rb, cb), BF),
            ((n_dp, n_t) + w_bc.shape, BF, IN_PLACE), ((n_dp, n_t) + pack.shape, F32, IN_PLACE),
        ],
        Gather.scratch(n_dp, n_t) * 3 + Deal.scratch(n_dp, pieces) + [dma(1), dma(1)],
    )
    u = u.reshape(micro, rows, width)
    wx = joined(wx)
    wbc = wbc.reshape(width, 2 * state)
    packs = packs.reshape(n_dp, n_t, total)
    cut = [packs[:, :, a:b] for a, b in zip(starts, starts[1:])]
    stacked = cut[0].reshape(n_dp, n_t, taps + 2, per_t, size_d).transpose(2, 1, 3, 0, 4)
    stacked = stacked.reshape(taps + 2, inner)
    gain = cut[1].reshape(1, width)
    bc_small = cut[2].reshape(n_dp * n_t, taps + 1, -1).transpose(1, 0, 2).reshape(taps + 1, 2 * state)
    wdt_p = pad_lanes(
        cut[3].reshape(n_dp, n_t, rb, per_t).transpose(0, 2, 1, 3).reshape(width, heads).astype(BF)
    )
    heads_f = cut[4][0].reshape(n_t, 3, per_t).transpose(1, 0, 2).reshape(3, heads)
    kx, bx, ngain = pad_rows(stacked[:taps]), stacked[taps : taps + 1], stacked[taps + 1 :]
    kbc_p, bbc = pad_rows(bc_small[:taps]), bc_small[taps:]
    dtb, alog = pad_lanes(heads_f[0:1]), pad_lanes(heads_f[1:2])
    dskip = jnp.repeat(heads_f[2], size)[None, :]

    nrm, xr, bcr, dtr, cum, xc, xh, bc, s_loc, dec = call(
        first_kernel, dims, micro, (lens, pos0), (u, halo),
        (gain, wx, wbc, wdt_p, kx, bx, kbc_p, bbc, dtb, alog),
        [
            ((micro, rows + HALO, width), BF, True),
            ((micro, rows + HALO, inner), BF, True),
            ((micro, rows + HALO, 2 * state), BF, True),
            ((micro, rows, LANES), F32, True),
            ((micro, rows, LANES), F32, True),
            ((micro, rows, inner), BF, True),
            ((micro, rows, inner), BF, True),
            ((micro, rows, 2 * state), BF, True),
            ((micro, state, inner), F32, True),
            ((micro, 8, inner), F32, True),
        ],
        [],
    )
    states = (micro, state, inner)
    g, hin, wz, wo = talk(
        ahead_kernel, n_dp, n_t, 2, (order, cotangent.reshape(pieces), w_z, w_out.T, s_loc, dec),
        [SCALARS, IN_VMEM, IN_PLACE, IN_PLACE, IN_VMEM, IN_VMEM],
        [
            (pieces, BF, IN_VMEM), (states, BF, IN_VMEM), gathered((rb, cb), BF),
            gathered((rb, cb), BF),
        ],
        Gather.scratch(n_dp, n_t) * 2 + Deal.scratch(n_dp, pieces) + Chain.scratch(states),
    )
    g = g.reshape(micro, rows, width)
    wz, wo = joined(wz), joined(wo)
    slot_shape = (n_dp, n_t, rb, cb)
    grad_shape = slot_shape if aligned else (width, inner)

    def parted(w):
        return w if aligned else w.reshape(n_dp, rb, n_t, cb).transpose(0, 2, 1, 3)

    out_rows, dz, dy, rd, ds_loc, dnz, dwo, dwz, dgain, ddskip = call(
        second_kernel, dims, micro, (lens, pos0), (nrm, cum, xc, xh, bc, hin, u, g),
        (wz, wo, ngain, dskip),
        [
            ((micro, rows, width), BF, True),
            ((micro, rows, inner), BF, True),
            ((micro, rows, inner), BF, True),
            ((micro, rows, LANES), F32, True),
            ((micro, state, inner), F32, True),
            ((micro, rows, width), F32, True),
            (grad_shape, BF, False),
            (grad_shape, BF, False),
            ((8, inner), F32, False),
            ((8, inner), F32, False),
        ],
        [
            ((rows, inner), F32), ((rows, inner), F32), ((rows, inner), F32), ((rows, inner), F32),
            ((rows, inner), BF), ((width, inner), F32), ((width, inner), F32),
        ],
    )
    output, dso, sum_z, sum_o = talk(
        behind_kernel, n_dp, n_t, 3,
        (deal, out_rows.reshape(pieces), parted(dwz), parted(dwo), ds_loc, dec),
        [SCALARS] + [IN_VMEM] * 5,
        [
            (pieces, BF, IN_VMEM), (states, BF, IN_VMEM), ((rb, cb), F32, IN_VMEM),
            ((rb, cb), F32, IN_VMEM),
        ],
        Scatter.scratch(n_dp, n_t, (rb, cb), BF) * 2 + Undeal.scratch(n_dp, pieces)
        + Chain.scratch(states),
    )
    dn, dwx, dwbc, dwdt, dkx, dkbc, ddt = call(
        third_kernel, dims, micro, (lens, pos0),
        (nrm, dtr, cum, xr, bcr, xh, bc, hin, s_loc, dec, dso, dy, rd, dnz),
        (wx, wbc, wdt_p, kx, bx, kbc_p, bbc, dtb, alog, dskip),
        [
            ((micro, rows + HALO, width), F32, True),
            (grad_shape, BF, False),
            ((width, 2 * state), F32, False),
            ((width, LANES), F32, False),
            ((8, inner), F32, False),
            ((8, 2 * state), F32, False),
            ((8, LANES), F32, False),
        ],
        [((width, inner), F32)],
    )
    back = [(i + 1, i) for i in range(n_t - 1)]
    spill = lax.ppermute(dn[:, :HALO, :], "tensor", back)
    dn = dn[:, HALO:, :] + jnp.pad(spill, [(0, 0), (rows - HALO, 0), (0, 0)])
    uf = u.astype(F32)
    q = lax.rsqrt(jnp.mean(uf * uf, axis=2, keepdims=True) + EPS)
    f = dn * gain[None]
    d_u = q * f - uf * (q * q * q) * (jnp.sum(f * uf, axis=2, keepdims=True) / width)
    d_pre = jnp.sum(dn * uf * q, axis=(0, 1))
    dtok_rows = (g.astype(F32) + d_u).astype(BF)

    stacked_g = jnp.concatenate([dkx[: taps + 1], dgain[0:1]], axis=0)
    stacked_g = stacked_g.reshape(taps + 2, n_t, per_t, n_dp, size_d).transpose(3, 1, 0, 2, 4)
    bc_g = dkbc[: taps + 1].reshape(taps + 1, n_dp, n_t, -1).transpose(1, 2, 0, 3)
    dt_g = dwdt[:, :heads].reshape(n_dp, rb, n_t, per_t).transpose(0, 2, 1, 3)
    heads_g = jnp.stack([ddt[0, :heads], ddt[1, :heads], ddskip[0].reshape(heads, size).sum(1)])
    heads_g = heads_g.reshape(3, n_t, per_t).transpose(1, 0, 2)
    heads_g = jnp.broadcast_to(heads_g[None], (n_dp,) + heads_g.shape)
    pack_g = jnp.concatenate(
        [
            stacked_g.reshape(n_dp, n_t, -1), d_pre.reshape(n_dp, n_t, -1),
            bc_g.reshape(n_dp, n_t, -1), dt_g.reshape(n_dp, n_t, -1),
            heads_g.reshape(n_dp, n_t, -1), jnp.zeros((n_dp, n_t, total - used), F32),
        ],
        axis=2,
    ).reshape((n_dp, n_t) + pack.shape)
    d_tokens, sum_x, d_wbc, sums = talk(
        leave_kernel, n_dp, n_t, 4,
        (
            deal, dtok_rows.reshape(pieces), parted(dwx),
            dwbc.astype(BF).reshape((n_dp, n_t) + w_bc.shape), pack_g,
        ),
        [SCALARS] + [IN_VMEM] * 4,
        [
            (pieces, BF, IN_VMEM), ((rb, cb), F32, IN_VMEM), (w_bc.shape, F32, IN_VMEM),
            (pack.shape, F32, IN_VMEM),
        ],
        Scatter.scratch(n_dp, n_t, pack.shape, F32) + Scatter.scratch(n_dp, n_t, w_bc.shape, BF)
        + Scatter.scratch(n_dp, n_t, (rb, cb), BF) + Undeal.scratch(n_dp, pieces),
    )
    sums = sums.reshape(total)
    got = [sums[a:b] for a, b in zip(starts, starts[1:])]
    got_stacked = got[0].reshape(taps + 2, per_t, size_d)
    got_bc = got[2].reshape(taps + 1, -1)
    got_heads = got[4].reshape(3, per_t)
    return (
        output.reshape(tokens.shape), d_tokens.reshape(tokens.shape), got[1], sum_z, sum_x, d_wbc,
        got[3].reshape(rb, per_t), got_stacked[:taps], got_stacked[taps], got_bc[:taps],
        got_bc[taps], got_heads[0], got_heads[1], got_heads[2], got_stacked[taps + 1], sum_o.T,
    )


def solution(mesh):
    both = ("dp", "tensor")
    in_specs = (
        P(None, both, None), P(None, "dp", None), P(None, "dp", None), P(None, both, None), P(both),
        P("dp", "tensor"), P("dp", "tensor"), P(both, None), P("dp", "tensor"),
        P(None, "tensor", "dp"), P("tensor", "dp"), P(None, both), P(both), P("tensor"),
        P("tensor"), P("tensor"), P("tensor", "dp"), P("tensor", "dp"),
    )
    out_specs = (
        P(None, both, None), P(None, both, None), P(both), P("dp", "tensor"), P("dp", "tensor"),
        P(both, None), P("dp", "tensor"), P(None, "tensor", "dp"), P("tensor", "dp"), P(None, both),
        P(both), P("tensor"), P("tensor"), P("tensor"), P("tensor", "dp"), P("tensor", "dp"),
    )
    return jax.shard_map(local, mesh=mesh, in_specs=in_specs, out_specs=out_specs, check_vma=False)
```
